256 devices in a mesh: expert: 64 (over z, x_lo, y), dp: 4 (over x_hi, core).
Axes of the slice: x: 4 (x_hi: 2, x_lo: 2; x = x_hi * 2 + x_lo), y: 4, z: 8, core: 2. Of those that a mesh axis runs over, the one named last changes fastest.
Arguments:
- tokens: bfloat16 [8192, 3584], P('expert', 'dp'), may hold values from -6 to 6
- expert_ids: int32 [8192, 8], P('expert'), may hold values from 0 to 127, as said below
- gate_weights: float32 [8192, 8], P('expert'), may hold values from 0.05 to 0.5
- replica_plan: int32 [64], replicated, may hold values from 0 to 127, as said below
- w_gate: bfloat16 [128, 3584, 1024], P('expert', None, 'dp'), may hold values from -0.09375 to 0.09375
- w_up: bfloat16 [128, 3584, 1024], P('expert', None, 'dp'), may hold values from -0.09375 to 0.09375
- w_down: bfloat16 [128, 1024, 3584], P('expert', 'dp'), may hold values from -0.1875 to 0.1875
Outputs:
- mixed_out: bfloat16 [8192, 3584], P('expert', 'dp')
The draws below stay inside these ranges and needn't reach their ends.
Inputs may be any that keep to these rules, and one draw needn't show every extreme that they name: `expert_ids`: each row names 8 different experts; one expert, which varies with the draw, is named by every row. `replica_plan`: entry j names one of the 2 experts owned by index (j + 32) % 64 of the expert axis, that is, an expert from k * 2 to k * 2 + 1 with that index k.
All inputs are finite; a program needn't handle non-finite values.
Results may differ from the reference program's by a relative error of at most 0.012.
Values may be sent and summed in bfloat16 or wider, within the bound.
A program may use at most 128 MiB of HBM per device.

```python
import math
import jax
import jax.numpy as jnp
from jax import lax

D = 3584
FF = 1024
EXP_DEV = 2
TOP = 8
CAP = 8
TOK_DEV = 128
OWNERS = 64
EXPERTS = 128
TOKENS = 8192
N_DP = 4


def hot_levels(key):
    shuffled = jax.random.permutation(jax.random.fold_in(key, 11), EXPERTS)
    position = jnp.zeros((EXPERTS,), jnp.int32).at[shuffled].set(jnp.arange(EXPERTS, dtype=jnp.int32))
    levels = jnp.where(position == 0, 64, jnp.where(position <= EXPERTS // 8, 2, jnp.where(position <= EXPERTS // 4, 1, 0)))
    return levels.astype(jnp.int32)


def draw_expert_ids(key, part):
    levels = hot_levels(key)
    noise_bits = jax.random.randint(jax.random.fold_in(key, 23), (TOKENS, EXPERTS), 0, 65536)
    scores = (noise_bits + levels[None, :] * 4096) * EXPERTS + jnp.arange(EXPERTS, dtype=jnp.int32)[None, :]
    return lax.top_k(scores, TOP)[1].astype(jnp.int32)


def draw_replica_plan(key, part):
    levels = hot_levels(key)
    owner_index = (jnp.arange(OWNERS, dtype=jnp.int32) + OWNERS // 2) % OWNERS
    candidate = owner_index[:, None] * EXP_DEV + jnp.arange(EXP_DEV, dtype=jnp.int32)[None, :]
    tiebreak = jax.random.randint(jax.random.fold_in(key, 31), (OWNERS, EXP_DEV), 0, 1024)
    scores = (levels[candidate] * 1024 + tiebreak) * EXP_DEV + jnp.arange(EXP_DEV, dtype=jnp.int32)[None, :]
    chosen = lax.top_k(scores, 1)[1][:, 0]
    return (owner_index * EXP_DEV + chosen).astype(jnp.int32)


def block_scale(rng, shape, split, smallest, largest):
    loudness, own = 1.0, jax.random.fold_in(rng, 6)
    for dim, blocks in split:
        heights = jnp.exp(jax.random.uniform(jax.random.fold_in(own, dim), (blocks,), jnp.float32, smallest / len(split), largest / len(split)))
        loudness = loudness * jnp.repeat(heights, shape[dim] // blocks).reshape([-1 if axis == dim else 1 for axis in range(len(shape))])
    return loudness


def bell_draw(key, dims, spread, limit, split=(), kind=jnp.bfloat16):
    result = jax.random.normal(key, dims, jnp.float32) * spread
    if len(split) > 0:
        result = block_scale(key, dims, split, -0.22, 0.18) * result
    return jnp.clip(result, min=-limit, max=limit).astype(kind)


def setup_inputs(seed: int = 0) -> dict:
    keys = jax.random.split(jax.random.key(seed), 8)
    return {
        "tokens": bell_draw(keys[0], (TOKENS, D), 1.0, 6.0, ((0, 64), (1, 4))),
        "expert_ids": draw_expert_ids(jax.random.fold_in(keys[7], 71), 0),
        "gate_weights": jnp.clip(jnp.exp(math.log(0.5) - 2.3025851 * jax.random.uniform(keys[2], (TOKENS, TOP), jnp.float32) ** block_scale(keys[2], (TOKENS, TOP), ((0, 64),), -0.2, 0.2)), 0.05, 0.5),
        "replica_plan": draw_replica_plan(jax.random.fold_in(keys[7], 71), 0),
        "w_gate": bell_draw(keys[4], (EXPERTS, D, FF), D ** -0.5, 0.09375, ((0, 64), (2, 4))),
        "w_up": bell_draw(keys[5], (EXPERTS, D, FF), D ** -0.5, 0.09375, ((0, 64), (2, 4))),
        "w_down": bell_draw(keys[6], (EXPERTS, FF, D), FF ** -0.5, 0.1875, ((0, 64), (1, 4))),
    }


def routing_tables(expert_ids, gate_weights, replica_plan):
    host_slots = EXP_DEV + 1
    per_block = TOK_DEV * TOP
    block_ids = expert_ids.reshape(OWNERS, per_block)
    expert_range = jnp.arange(EXPERTS, dtype=jnp.int32)
    onehot = (block_ids[:, :, None] == expert_range[None, None, :]).astype(jnp.int32)
    row_rank = jnp.sum((jnp.cumsum(onehot, axis=1) - onehot) * onehot, axis=2)
    hosted = (replica_plan[:, None] == expert_range[None, :]).astype(jnp.int32)
    copies = 1 + jnp.sum(hosted, axis=0)
    host_of = jnp.sum(jnp.arange(OWNERS, dtype=jnp.int32)[:, None] * hosted, axis=0)
    my_copies = copies[block_ids]
    my_host = host_of[block_ids]
    copy_index = row_rank % my_copies
    position = row_rank // my_copies
    is_kept = position < CAP
    target = jnp.where(copy_index == 0, block_ids // EXP_DEV, my_host)
    target_slot = jnp.where(copy_index == 0, block_ids % EXP_DEV, EXP_DEV)
    sender = jnp.arange(OWNERS, dtype=jnp.int32)[:, None]
    buffer_rows = OWNERS * host_slots * OWNERS * CAP
    slot_place = jnp.where(is_kept, ((target * host_slots + target_slot) * OWNERS + sender) * CAP + position, buffer_rows)
    token_row = sender * TOK_DEV + jnp.arange(per_block, dtype=jnp.int32)[None, :] // TOP
    table = jnp.full((buffer_rows,), TOKENS, jnp.int32).at[slot_place.reshape(-1)].set(token_row.reshape(-1), mode="drop")
    weight_table = jnp.zeros((buffer_rows,), jnp.float32).at[slot_place.reshape(-1)].set(gate_weights.reshape(-1), mode="drop")
    return table, weight_table


def expert_rows(slot_rows, expert, w_gate, w_up, w_down):
    quarter = FF // N_DP
    gate_full = w_gate[expert]
    up_full = w_up[expert]
    down_full = w_down[expert]
    running = jnp.zeros((slot_rows.shape[0], D), jnp.float32)
    for part_number in range(N_DP):
        start_col = part_number * quarter
        stop_col = start_col + quarter
        gate_value = jnp.dot(slot_rows, gate_full[:, start_col:stop_col], preferred_element_type=jnp.float32)
        up_value = jnp.dot(slot_rows, up_full[:, start_col:stop_col], preferred_element_type=jnp.float32)
        hidden = (jax.nn.silu(gate_value) * up_value).astype(jnp.bfloat16)
        partial_value = jnp.dot(hidden, down_full[start_col:stop_col, :], preferred_element_type=jnp.float32).astype(jnp.bfloat16)
        partial_value = lax.optimization_barrier(partial_value)
        running = running + partial_value.astype(jnp.float32)
    return running


def reference(tokens, expert_ids, gate_weights, replica_plan, w_gate, w_up, w_down):
    table, weight_table = routing_tables(expert_ids, gate_weights, replica_plan)
    host_slots = EXP_DEV + 1
    padded = jnp.concatenate([tokens, jnp.zeros((1, D), tokens.dtype)], axis=0)
    owned = jnp.arange(OWNERS, dtype=jnp.int32)[:, None] * EXP_DEV + jnp.arange(EXP_DEV, dtype=jnp.int32)[None, :]
    slot_expert = jnp.concatenate([owned, replica_plan[:, None]], axis=1).reshape(-1)
    slot_tables = table.reshape(OWNERS * host_slots, OWNERS * CAP)
    slot_weights = weight_table.reshape(OWNERS * host_slots, OWNERS * CAP)

    def visit(running, inputs):
        rows_index, row_weights, expert = inputs
        values = expert_rows(padded[rows_index], expert, w_gate, w_up, w_down)
        return running.at[rows_index].add(values * row_weights[:, None]), None

    start = jnp.zeros((TOKENS + 1, D), jnp.float32)
    mixed_out, unused = lax.scan(visit, start, (slot_tables, slot_weights, slot_expert))
    return mixed_out[:TOKENS].astype(jnp.bfloat16)
```

```python
import jax
import jax.numpy as jnp
from jax import lax
from jax.sharding import PartitionSpec as P

CAP = 8


def per_device(tokens, expert_ids, gate_weights, replica_plan, w_gate, w_up, w_down):
    owners = lax.axis_size("expert")
    me = lax.axis_index("expert")
    owned = w_gate.shape[0]
    experts = owned * owners
    rows = (owned + 1) * CAP
    tok, feat = tokens.shape
    width = w_gate.shape[1]
    expert_range = jnp.arange(experts, dtype=jnp.int32)
    hit = expert_ids[:, :, None] == expert_range[None, None, :]
    member = jnp.any(hit, axis=1)
    gate = jnp.sum(jnp.where(hit, gate_weights[:, :, None], 0.0), axis=1)
    earlier = jnp.tri(tok, tok, -1, dtype=jnp.bfloat16)
    rank = jnp.dot(earlier, member.astype(jnp.bfloat16), preferred_element_type=jnp.float32)
    key = jnp.where(member, rank.astype(jnp.int32), -1).reshape(tok, owners, owned)
    gate = gate.reshape(tok, owners, owned)
    owner_range = jnp.arange(owners, dtype=jnp.int32)
    planned = jnp.roll(replica_plan, owners // 2) - owner_range * owned
    second = (planned == 1)[None, :]
    key3 = jnp.stack([key[..., 0], key[..., 1], jnp.where(second, key[..., 1], key[..., 0]) - CAP], 2)
    gate3 = jnp.stack([gate[..., 0], gate[..., 1], jnp.where(second, gate[..., 1], gate[..., 0])], 2)
    place = jnp.arange(CAP, dtype=jnp.int32)
    chosen = key3[..., None] == place
    select = chosen.astype(jnp.bfloat16).reshape(tok, owners * rows)
    mix = jnp.where(chosen, gate3[..., None], 0.0).reshape(tok, owners * rows)
    outgoing = lax.dot_general(
        select, tokens, (((0,), (0,)), ((), ())), preferred_element_type=jnp.bfloat16
    ).reshape(owners, rows, feat)
    arrived = lax.all_to_all(outgoing, "expert", split_axis=0, concat_axis=0, tiled=True)
    full = lax.all_gather(arrived.reshape(owners * rows, feat), "dp", axis=0, tiled=False)
    n_dp = full.shape[0]
    full = full.transpose(1, 0, 2).reshape(owners, owned + 1, CAP, width)
    mine = planned[me]
    outs = []
    for slot in range(owned + 1):
        x = full[:, slot].reshape(owners * CAP, width)
        pick = slot if slot < owned else mine
        wg = lax.dynamic_index_in_dim(w_gate, pick, 0, keepdims=False)
        wu = lax.dynamic_index_in_dim(w_up, pick, 0, keepdims=False)
        wd = lax.dynamic_index_in_dim(w_down, pick, 0, keepdims=False)
        g = jnp.dot(x, wg, preferred_element_type=jnp.float32)
        u = jnp.dot(x, wu, preferred_element_type=jnp.float32)
        h = (jax.nn.silu(g) * u).astype(jnp.bfloat16)
        o = jnp.dot(h, wd, preferred_element_type=jnp.float32).astype(jnp.bfloat16)
        outs.append(o.reshape(owners, CAP, width))
    partial = jnp.stack(outs, axis=1).reshape(owners * rows, n_dp, feat).transpose(1, 0, 2)
    summed = lax.psum_scatter(partial, "dp", scatter_dimension=0, tiled=False)
    back = lax.all_to_all(
        summed.reshape(owners, rows, feat), "expert", split_axis=0, concat_axis=0, tiled=True
    ).reshape(owners * rows, feat)
    high = mix.astype(jnp.bfloat16)
    low = (mix - high.astype(jnp.float32)).astype(jnp.bfloat16)
    out = jnp.dot(high, back, preferred_element_type=jnp.float32)
    out = out + jnp.dot(low, back, preferred_element_type=jnp.float32)
    return out.astype(jnp.bfloat16)


def solution(mesh):
    in_specs = (
        P("expert", "dp"),
        P("expert", None),
        P("expert", None),
        P(),
        P("expert", None, "dp"),
        P("expert", None, "dp"),
        P("expert", "dp", None),
    )
    return jax.shard_map(
        per_device, mesh=mesh, in_specs=in_specs, out_specs=P("expert", "dp"), check_vma=False
    )
```

```python
import functools

import jax
import jax.numpy as jnp
from jax import lax
from jax.experimental import pallas as pl
from jax.experimental.pallas import tpu as pltpu
from jax.sharding import PartitionSpec as P

CAP = 8
N_LO, N_Y, N_HI, N_CORE = 2, 4, 2, 2
N_X = N_LO * N_HI
GROUPS = 3
ROWS = GROUPS * 2 * CAP
CHUNKS = ((0, 1), (-2, 3), (-3, 4), (-1, 2))
BF16, F32 = jnp.bfloat16, jnp.float32


def kernel(
    n_z, tok_ref, meta_ref, plan_ref, wg_hbm, wu_hbm, wd_hbm, out_ref,
    wg, wu, wd, toks, metas, picks, mix_hi, mix_lo, g_buf, y_in, x_buf, relay, core_in,
    x_back, relay_back, y_out, y_back, z_out, z_back,
    send_sem, recv_sem, local_sem,
):
    expert = lax.axis_index("expert")
    dp = lax.axis_index("dp")
    z, lo, y = expert // (N_LO * N_Y), (expert // N_Y) % N_LO, expert % N_Y
    hi, core = dp // N_CORE, dp % N_CORE
    x = hi * N_LO + lo
    n_tok = tok_ref.shape[0]
    feat = tok_ref.shape[1]
    hidden = wg.shape[2]
    n_chunk = len(CHUNKS)

    def device(z_, x_, y_, core_):
        return ((z_ * N_LO + x_ % N_LO) * N_Y + y_, (x_ // N_LO) * N_CORE + core_)

    def along_z(step):
        return device((z + step + n_z) % n_z, x, y, core)

    def along_y(step):
        return device(z, x, (y + step) % N_Y, core)

    def along_x(step):
        return device(z, (x + step) % N_X, y, core)

    right, left = (x + 1) % N_X, (x + N_X - 1) % N_X
    across = (x + 2) % N_X
    partner = device(z, x, y, 1 - core)

    started = []
    count = [0]
    local_count = [0]

    def remote(src, dst, target):
        i = count[0]
        count[0] += 1
        copy = pltpu.make_async_remote_copy(
            src_ref=src, dst_ref=dst, send_sem=send_sem.at[i], recv_sem=recv_sem.at[i],
            device_id=target, device_id_type=pl.DeviceIdType.MESH,
        )
        copy.start()
        started.append(copy)
        return copy

    def local(src, dst):
        i = local_count[0]
        local_count[0] += 1
        copy = pltpu.make_async_copy(src, dst, local_sem.at[i])
        copy.start()
        return copy

    def received(copies):
        for c in copies:
            c.wait_recv()

    def sent(copies):
        for c in copies:
            c.wait_send()
            started[:] = [other for other in started if other is not c]

    weight_loads = [
        local(wg_hbm, wg.at[pl.ds(0, 2)]),
        local(wu_hbm, wu.at[pl.ds(0, 2)]),
        local(wd_hbm, wd.at[pl.ds(0, 2)]),
    ]
    where = {d: (c, j) for c, pair in enumerate(CHUNKS) for j, d in enumerate(pair)}
    own_loads = [local(tok_ref, toks.at[where[0]]), local(meta_ref, metas.at[where[0]])]

    barrier = pltpu.get_barrier_semaphore()
    peers = [along_z(s) for s in range(1, n_z)] + [along_y(s) for s in range(1, N_Y)]
    peers += [along_x(1), along_x(3), partner]
    for peer in peers:
        pl.semaphore_signal(barrier, inc=1, device_id=peer, device_id_type=pl.DeviceIdType.MESH)
    pl.semaphore_wait(barrier, len(peers))

    z_in = {}

    def z_forward(d):
        step = 1 if d > 0 else -1
        for s in ((step,) if d else (1, -1)):
            if d:
                received(z_in[d])
                src_t, src_m = toks.at[where[d]], metas.at[where[d]]
            else:
                src_t, src_m = tok_ref, meta_ref
            nxt = d + s
            if nxt in where:
                z_in[nxt] = [
                    remote(src_t, toks.at[where[nxt]], along_z(-s)),
                    remote(src_m, metas.at[where[nxt]], along_z(-s)),
                ]

    before = (
        lax.broadcasted_iota(jnp.int32, (n_tok, n_tok), 0)
        < lax.broadcasted_iota(jnp.int32, (n_tok, n_tok), 1)
    ).astype(F32).astype(BF16)
    plane = N_LO * N_Y
    place = lax.broadcasted_iota(jnp.int32, (CAP, n_tok), 0).astype(F32)
    blank = jnp.zeros((CAP, n_tok), F32)

    def planned_of(owner):
        owners = n_z * plane
        return (plan_ref[(owner + owners // 2) % owners] - 2 * owner).astype(F32)

    def slots(c):
        keys, gates = [], []
        ids = lax.broadcasted_iota(jnp.int32, (2 * plane, n_tok), 0) + z * (2 * plane)
        ids = ids.astype(F32)
        for j in range(2):
            meta = metas[c, j]
            member = jnp.zeros((2 * plane, n_tok), F32)
            gate = jnp.zeros((2 * plane, n_tok), F32)
            for k in range(8):
                hit = meta[k : k + 1, :] == ids
                member = jnp.where(hit, 1.0, member)
                gate = jnp.where(hit, meta[8 + k : 9 + k, :], gate)
            rank = jnp.dot(member.astype(BF16), before, preferred_element_type=F32)
            keys.append(jnp.where(member > 0.5, rank, -1.0))
            gates.append(gate)
        for yy in range(N_Y):
            for ll in range(N_LO):
                r = ll * (2 * N_Y) + yy * 2
                f = planned_of(z * plane + ll * N_Y + yy)
                base = (yy * N_LO + ll) * ROWS
                for g in range(GROUPS):
                    ones, weights = [], []
                    for j in range(2):
                        k0, k1 = keys[j][r : r + 1, :], keys[j][r + 1 : r + 2, :]
                        w0, w1 = gates[j][r : r + 1, :], gates[j][r + 1 : r + 2, :]
                        if g == 0:
                            k, w = k0, w0
                        elif g == 1:
                            k, w = k1, w1
                        else:
                            k = k0 * (1.0 - f) + k1 * f - float(CAP)
                            w = w0 * (1.0 - f) + w1 * f
                        hit = jnp.broadcast_to(k, (CAP, n_tok)) == place
                        one = jnp.where(hit, 1.0, 0.0)
                        weight = jnp.where(hit, jnp.broadcast_to(w, (CAP, n_tok)), 0.0)
                        row1 = [blank, blank]
                        row2 = [blank, blank]
                        row1[j], row2[j] = one, weight
                        ones.append(jnp.concatenate(row1, axis=1))
                        weights.append(jnp.concatenate(row2, axis=1))
                    at = pl.ds(base + g * 2 * CAP, 2 * CAP)
                    picks[at, :] = jnp.concatenate(ones, axis=0).astype(BF16)
                    w = jnp.concatenate(weights, axis=0)
                    high = w.astype(BF16)
                    mix_hi[c, at, :] = high
                    mix_lo[c, at, :] = (w - high.astype(F32)).astype(BF16)

    y_moves, x_moves, x_relays, x_fwd, core_moves, own_moves = {}, {}, {}, {}, {}, {}
    reduce_moves, b_moves, b_relays, b_fwd, yb_moves, zb_moves = {}, {}, {}, {}, {}, {}

    def d1(c):
        slots(c)
        both = toks[c].reshape(2 * n_tok, feat)
        rows = jnp.dot(picks[...], both, preferred_element_type=F32).astype(BF16)
        g_buf[c] = rows.reshape(N_Y, N_LO, ROWS, feat)
        y_moves[c] = [
            remote(g_buf.at[c, (y + s) % N_Y], y_in.at[c, :, y], along_y(s)) for s in (2, 1, 3)
        ]
        own_moves[c] = local(g_buf.at[c, y], y_in.at[c, :, y])

    half = N_Y // 2

    def d2(c):
        own_moves[c].wait()
        received(y_moves[c])
        mine = y_in.at[c, lo]
        x_relays[c] = [
            remote(mine.at[pl.ds(0, half)], relay.at[c, 0], along_x(1)),
            remote(mine.at[pl.ds(half, half)], relay.at[c, 1], along_x(3)),
        ]
        x_moves[c] = [
            remote(y_in.at[c, 1 - lo], x_buf.at[c, hi, core, lo], along_x(1)),
            remote(y_in.at[c, 1 - lo], x_buf.at[c, hi, core, lo], along_x(3)),
        ]
        core_moves[c] = [remote(mine, x_buf.at[c, hi, core, lo], partner)]
        own_moves[c] = local(mine, x_buf.at[c, hi, core, lo])

    def d3(c):
        received(x_relays[c])
        x_fwd[c] = [
            remote(relay.at[c, 0], x_buf.at[c, left // N_LO, core, 1 - lo, pl.ds(0, half)], along_x(1)),
            remote(relay.at[c, 1], x_buf.at[c, right // N_LO, core, 1 - lo, pl.ds(half, half)], along_x(3)),
        ]

    def d4(c):
        received(x_moves[c])
        for other in (left, right):
            block = x_buf.at[c, other // N_LO, core, 1 - lo]
            core_moves[c].append(remote(block, block, partner))
        received(x_fwd[c])
        block = x_buf.at[c, across // N_LO, core, lo]
        core_moves[c].append(remote(block, block, partner))

    def d5(c):
        own_moves[c].wait()
        received(core_moves[c])
        sent(core_moves[c])

        def group(g, carry):
            at = pl.ds(pl.multiple_of(g * 2 * CAP, 2 * CAP), 2 * CAP)
            m = N_LO * N_Y * 2 * CAP
            gate = jnp.zeros((m, hidden), F32)
            up = jnp.zeros((m, hidden), F32)
            for q in range(4):
                rows = x_buf[c, q // 2, q % 2, :, :, at, :].reshape(m, feat)
                ks = pl.ds(q * feat, feat)
                gate += jnp.dot(rows, wg[g, ks, :], preferred_element_type=F32)
                up += jnp.dot(rows, wu[g, ks, :], preferred_element_type=F32)
            h = (gate / (1.0 + jnp.exp(-gate)) * up).astype(BF16)
            for q in range(4):
                o = jnp.dot(h, wd[g, :, pl.ds(q * feat, feat)], preferred_element_type=F32)
                x_buf[c, q // 2, q % 2, :, :, at, :] = o.astype(BF16).reshape(
                    N_LO, N_Y, 2 * CAP, feat
                )
            return carry

        lax.fori_loop(0, GROUPS, group, 0)
        reduce_moves[c] = remote(x_buf.at[c, :, 1 - core], core_in.at[c], partner)

    def r1(c):
        received([reduce_moves[c]])

        def add(i, carry):
            h_, s_, y_ = i // (N_LO * N_Y), (i // N_Y) % N_LO, i % N_Y
            total = x_buf[c, h_, core, s_, y_].astype(F32) + core_in[c, h_, s_, y_].astype(F32)
            x_buf[c, h_, core, s_, y_] = total.astype(BF16)
            return carry

        lax.fori_loop(0, N_HI * N_LO * N_Y, add, 0)
        far = x_buf.at[c, across // N_LO, core, lo]
        b_relays[c] = [
            remote(far.at[pl.ds(0, half)], relay_back.at[c, 0], along_x(1)),
            remote(far.at[pl.ds(half, half)], relay_back.at[c, 1], along_x(3)),
        ]
        b_moves[c] = [
            remote(x_buf.at[c, right // N_LO, core, 1 - lo], x_back.at[c, 0], along_x(1)),
            remote(x_buf.at[c, left // N_LO, core, 1 - lo], x_back.at[c, 1], along_x(3)),
        ]

    def r2(c):
        received(b_relays[c])
        b_fwd[c] = [
            remote(relay_back.at[c, 0], x_back.at[c, 2, pl.ds(0, half)], along_x(1)),
            remote(relay_back.at[c, 1], x_back.at[c, 2, pl.ds(half, half)], along_x(3)),
        ]

    def r3(c):
        received(b_moves[c])
        received(b_fwd[c])

        def add(i, carry):
            y_out[c, 1 - lo, i] = (x_back[c, 0, i].astype(F32) + x_back[c, 1, i].astype(F32)).astype(BF16)
            y_out[c, lo, i] = (x_buf[c, hi, core, lo, i].astype(F32) + x_back[c, 2, i].astype(F32)).astype(BF16)
            return carry

        lax.fori_loop(0, N_Y, add, 0)
        yb_moves[c] = [
            remote(y_out.at[c, :, (y + s) % N_Y], y_back.at[c, y], along_y(s)) for s in (2, 1, 3)
        ]
        own_moves[c] = local(y_out.at[c, :, y], y_back.at[c, y])

    def r4(c):
        own_moves[c].wait()
        received(yb_moves[c])
        rows = y_back[c].reshape(N_Y * N_LO * ROWS, feat)
        dims = (((0,), (0,)), ((), ()))
        total = lax.dot_general(mix_hi[c], rows, dims, preferred_element_type=F32)
        total = total + lax.dot_general(mix_lo[c], rows, dims, preferred_element_type=F32)
        z_out[c] = total.astype(BF16).reshape(2, n_tok, feat)
        for j, d in enumerate(CHUNKS[c]):
            if d:
                zb_moves[c, j] = remote(z_out.at[c, j], z_back.at[c, j], along_z(d))
            else:
                own_z.append(local(z_out.at[c, j], z_back.at[c, j]))

    own_z = []

    def load_weights():
        for load in weight_loads:
            load.wait()
        f = planned_of(expert)

        def pick_rows(i, carry):
            at = pl.ds(pl.multiple_of(i * 128, 128), 128)
            for w in (wg, wu):
                w[2, at, :] = (w[0, at, :].astype(F32) * (1.0 - f) + w[1, at, :].astype(F32) * f).astype(BF16)
            return carry

        lax.fori_loop(0, wg.shape[1] // 128, pick_rows, 0)

        def pick_down(i, carry):
            at = pl.ds(pl.multiple_of(i * 16, 16), 16)
            wd[2, at, :] = (wd[0, at, :].astype(F32) * (1.0 - f) + wd[1, at, :].astype(F32) * f).astype(BF16)
            return carry

        lax.fori_loop(0, hidden // 16, pick_down, 0)

    z_forward(0)
    z_forward(1)
    z_forward(-1)
    for load in own_loads:
        load.wait()
    d1(0)
    load_weights()
    z_forward(2)
    z_forward(-2)
    d2(0)
    z_forward(3)
    z_forward(-3)
    d1(1)
    d3(0)
    z_forward(4)
    d1(2)
    d2(1)
    d4(0)
    d1(3)
    d3(1)
    d5(0)
    d2(2)
    d4(1)
    r1(0)
    d3(2)
    d5(1)
    d2(3)
    d4(2)
    r1(1)
    r2(0)
    d3(3)
    d5(2)
    r3(0)
    d4(3)
    r1(2)
    r2(1)
    d5(3)
    r1(3)
    r2(2)
    r3(1)
    r4(0)
    r2(3)
    r3(2)
    r4(1)
    r3(3)
    r4(2)
    r4(3)
    for copy in own_z:
        copy.wait()
    received(zb_moves.values())

    def finish(i, carry):
        at = pl.ds(pl.multiple_of(i * 16, 16), 16)
        total = jnp.zeros((16, feat), F32)
        for c in range(n_chunk):
            for j in range(2):
                total = total + z_back[c, j, at, :].astype(F32)
        out_ref[at, :] = total.astype(out_ref.dtype)
        return carry

    lax.fori_loop(0, n_tok // 16, finish, 0)
    sent(list(started))


N_REMOTE = 14 + 4 * (3 + 6 + 4 + 1 + 6 + 3) + 7
N_LOCAL = 5 + 4 * 3 + 1


def per_device(tokens, expert_ids, gate_weights, replica_plan, w_gate, w_up, w_down):
    owners = lax.axis_size("expert")
    n_z = owners // (N_LO * N_Y)
    tok, feat = tokens.shape
    width = w_gate.shape[1]
    hidden = w_gate.shape[2]
    meta = jnp.concatenate([expert_ids.T.astype(F32), gate_weights.T], axis=0)
    n_chunk = len(CHUNKS)
    vmem = pl.BlockSpec(memory_space=pltpu.VMEM)
    hbm = pl.BlockSpec(memory_space=pl.ANY)
    block = (N_Y, ROWS, feat)
    slot_rows = N_Y * N_LO * ROWS
    return pl.pallas_call(
        functools.partial(kernel, n_z),
        out_shape=jax.ShapeDtypeStruct((tok, feat), BF16),
        in_specs=[vmem, vmem, pl.BlockSpec(memory_space=pltpu.SMEM), hbm, hbm, hbm],
        out_specs=vmem,
        scratch_shapes=[
            pltpu.VMEM((3, width, hidden), BF16),
            pltpu.VMEM((3, width, hidden), BF16),
            pltpu.VMEM((3, hidden, width), BF16),
            pltpu.VMEM((n_chunk, 2, tok, feat), BF16),
            pltpu.VMEM((n_chunk, 2, 16, tok), F32),
            pltpu.VMEM((slot_rows, 2 * tok), BF16),
            pltpu.VMEM((n_chunk, slot_rows, 2 * tok), BF16),
            pltpu.VMEM((n_chunk, slot_rows, 2 * tok), BF16),
            pltpu.VMEM((n_chunk, N_Y, N_LO, ROWS, feat), BF16),
            pltpu.VMEM((n_chunk, N_LO) + block, BF16),
            pltpu.VMEM((n_chunk, N_HI, N_CORE, N_LO) + block, BF16),
            pltpu.VMEM((n_chunk, 2, N_Y // 2, ROWS, feat), BF16),
            pltpu.VMEM((n_chunk, N_HI, N_LO) + block, BF16),
            pltpu.VMEM((n_chunk, 3) + block, BF16),
            pltpu.VMEM((n_chunk, 2, N_Y // 2, ROWS, feat), BF16),
            pltpu.VMEM((n_chunk, N_LO) + block, BF16),
            pltpu.VMEM((n_chunk, N_Y, N_LO, ROWS, feat), BF16),
            pltpu.VMEM((n_chunk, 2, tok, feat), BF16),
            pltpu.VMEM((n_chunk, 2, tok, feat), BF16),
            pltpu.SemaphoreType.DMA((N_REMOTE,)),
            pltpu.SemaphoreType.DMA((N_REMOTE,)),
            pltpu.SemaphoreType.DMA((N_LOCAL,)),
        ],
        compiler_params=pltpu.CompilerParams(
            collective_id=0, has_side_effects=True, vmem_limit_bytes=67043328
        ),
    )(tokens, meta, replica_plan, w_gate, w_up, w_down)


def solution(mesh):
    in_specs = (
        P("expert", "dp"),
        P("expert", None),
        P("expert", None),
        P(),
        P("expert", None, "dp"),
        P("expert", None, "dp"),
        P("expert", "dp", None),
    )
    return jax.shard_map(
        per_device, mesh=mesh, in_specs=in_specs, out_specs=P("expert", "dp"), check_vma=False
    )
```

```python
import functools

import jax
import jax.numpy as jnp
from jax import lax
from jax.experimental import pallas as pl
from jax.experimental.pallas import tpu as pltpu
from jax.sharding import PartitionSpec as P

CAP = 8
N_LO, N_Y, N_HI, N_CORE = 2, 4, 2, 2
N_X = N_LO * N_HI
GROUPS = 3
ROWS = GROUPS * 2 * CAP
CHUNKS = ((1, -1), (2, -2), (3, -3), (0, 4))
PIECES = (1, 1, 1, 2)
BF16, F32 = jnp.bfloat16, jnp.float32


def kernel(
    n_z, tok_ref, ids_ref, gate_ref, plan_ref, wg_hbm, wu_hbm, wd_hbm, out_ref,
    wg, wu, wd, toks, metas, meta_own, picks, mix_hi, mix_lo, g_buf, g_far, y_in, x_buf, core_in,
    x_back, y_out, y_back, z_out, z_back,
    send_sem, recv_sem, local_sem,
):
    expert = lax.axis_index("expert")
    dp = lax.axis_index("dp")
    z, lo, y = expert // (N_LO * N_Y), (expert // N_Y) % N_LO, expert % N_Y
    hi, core = dp // N_CORE, dp % N_CORE
    x = hi * N_LO + lo
    n_tok = tok_ref.shape[0]
    feat = tok_ref.shape[1]
    hidden = wg.shape[2]
    n_chunk = len(CHUNKS)

    def device(z_, x_, y_, core_):
        return ((z_ * N_LO + x_ % N_LO) * N_Y + y_, (x_ // N_LO) * N_CORE + core_)

    def along_z(step):
        return device((z + step + n_z) % n_z, x, y, core)

    def along_y(step):
        return device(z, x, (y + step) % N_Y, core)

    def along_x(step):
        return device(z, (x + step) % N_X, y, core)

    right, left = (x + 1) % N_X, (x + N_X - 1) % N_X
    across = (x + 2) % N_X
    partner = device(z, x, y, 1 - core)

    started = []
    count = [0]
    local_count = [0]

    def remote(src, dst, target):
        i = count[0]
        count[0] += 1
        copy = pltpu.make_async_remote_copy(
            src_ref=src, dst_ref=dst, send_sem=send_sem.at[i], recv_sem=recv_sem.at[i],
            device_id=target, device_id_type=pl.DeviceIdType.MESH,
        )
        copy.start()
        started.append(copy)
        return copy

    def local(src, dst):
        i = local_count[0]
        local_count[0] += 1
        copy = pltpu.make_async_copy(src, dst, local_sem.at[i])
        copy.start()
        return copy

    def received(copies):
        for c in copies:
            c.wait_recv()

    def sent(copies):
        for c in copies:
            c.wait_send()
            started[:] = [other for other in started if other is not c]

    weight_loads = [
        local(wg_hbm, wg.at[pl.ds(0, 2)]),
        local(wu_hbm, wu.at[pl.ds(0, 2)]),
        local(wd_hbm, wd.at[pl.ds(0, 2)]),
    ]
    where = {d: (c, j) for c, pair in enumerate(CHUNKS) for j, d in enumerate(pair)}

    def tok_at(d, h):
        c, j = where[d]
        return toks.at[c, h, j]

    own_loads = [local(tok_ref, tok_at(0, hi))]
    meta_own[pl.ds(0, 8), :] = ids_ref[...].astype(F32)
    meta_own[pl.ds(8, 8), :] = gate_ref[...]
    metas[where[0]] = meta_own[...]

    barrier = pltpu.get_barrier_semaphore()
    peers = [along_z(s) for s in range(1, n_z)] + [along_y(s) for s in range(1, N_Y)]
    peers += [along_x(1), along_x(2), along_x(3), partner]
    for peer in peers:
        pl.semaphore_signal(barrier, inc=1, device_id=peer, device_id_type=pl.DeviceIdType.MESH)
    pl.semaphore_wait(barrier, len(peers))

    z_in, z_meta = {}, {}

    def z_near(d):
        for s in ((1, -1) if d == 0 else (1,) if d > 0 else (-1,)):
            if d:
                received([z_in[d, 0], z_meta[d]])
            nxt = d + s
            if nxt in where:
                src = tok_at(d, hi) if d else tok_ref
                src_m = metas.at[where[d]] if d else meta_own
                z_in[nxt, 0] = remote(src, tok_at(nxt, hi), along_z(-s))
                z_meta[nxt] = remote(src_m, metas.at[where[nxt]], along_z(-s))

    def z_far(d):
        received([z_in[d, 1]])
        for s in ((1, -1) if d == 0 else (1,) if d > 0 else (-1,)):
            nxt = d + s
            if nxt in where:
                z_in[nxt, 1] = remote(tok_at(d, 1 - hi), tok_at(nxt, 1 - hi), along_z(-s))

    def swap():
        z_in[0, 1] = remote(tok_ref, tok_at(0, hi), along_x(2))

    before = (
        lax.broadcasted_iota(jnp.int32, (n_tok, n_tok), 0)
        < lax.broadcasted_iota(jnp.int32, (n_tok, n_tok), 1)
    ).astype(F32).astype(BF16)
    plane = N_LO * N_Y
    place = lax.broadcasted_iota(jnp.int32, (CAP, n_tok), 0).astype(F32)
    blank = jnp.zeros((CAP, n_tok), F32)

    def planned_of(owner):
        owners = n_z * plane
        return (plan_ref[(owner + owners // 2) % owners] - 2 * owner).astype(F32)

    def slots(c):
        keys, gates = [], []
        ids = lax.broadcasted_iota(jnp.int32, (2 * plane, n_tok), 0) + z * (2 * plane)
        ids = ids.astype(F32)
        for j in range(2):
            meta = metas[c, j]
            member = jnp.zeros((2 * plane, n_tok), F32)
            gate = jnp.zeros((2 * plane, n_tok), F32)
            for k in range(8):
                hit = meta[k : k + 1, :] == ids
                member = jnp.where(hit, 1.0, member)
                gate = jnp.where(hit, meta[8 + k : 9 + k, :], gate)
            rank = jnp.dot(member.astype(BF16), before, preferred_element_type=F32)
            keys.append(jnp.where(member > 0.5, rank, -1.0))
            gates.append(gate)
        for yy in range(N_Y):
            for ll in range(N_LO):
                r = ll * (2 * N_Y) + yy * 2
                f = planned_of(z * plane + ll * N_Y + yy)
                base = (ll * N_Y + yy) * ROWS
                for g in range(GROUPS):
                    ones, weights = [], []
                    for j in range(2):
                        k0, k1 = keys[j][r : r + 1, :], keys[j][r + 1 : r + 2, :]
                        w0, w1 = gates[j][r : r + 1, :], gates[j][r + 1 : r + 2, :]
                        if g == 0:
                            k, w = k0, w0
                        elif g == 1:
                            k, w = k1, w1
                        else:
                            k = k0 * (1.0 - f) + k1 * f - float(CAP)
                            w = w0 * (1.0 - f) + w1 * f
                        hit = jnp.broadcast_to(k, (CAP, n_tok)) == place
                        one = jnp.where(hit, 1.0, 0.0)
                        weight = jnp.where(hit, jnp.broadcast_to(w, (CAP, n_tok)), 0.0)
                        row1 = [blank, blank]
                        row2 = [blank, blank]
                        row1[j], row2[j] = one, weight
                        ones.append(jnp.concatenate(row1, axis=1))
                        weights.append(jnp.concatenate(row2, axis=1))
                    at = pl.ds(base + g * 2 * CAP, 2 * CAP)
                    picks[c, at, :] = jnp.concatenate(ones, axis=0).astype(BF16)
                    w = jnp.concatenate(weights, axis=0)
                    high = w.astype(BF16)
                    mix_hi[c, at, :] = high
                    mix_lo[c, at, :] = (w - high.astype(F32)).astype(BF16)

    q_moves, p_moves, f_moves, x_moves, core_moves, own_moves = {}, {}, {}, {}, {}, {}
    reduce_moves, b_moves, yb_moves, zb_moves = {}, {}, {}, {}
    n_rows = N_Y * ROWS

    def to_planes(key, src, dst):
        moves = [remote(src((y + s) % N_Y), dst, along_y(s)) for s in (2, 1, 3)]
        own_moves[key] = local(src(y), dst)
        return moves

    def d1(c):
        slots(c)
        both = toks[c, hi].reshape(2 * n_tok, feat)
        rows = jnp.dot(picks[c], both, preferred_element_type=F32).astype(BF16)
        g_buf[c] = rows.reshape(N_LO, N_Y, ROWS, feat)
        q_moves[c] = to_planes((c, "q"), lambda t: g_buf.at[c, 1 - lo, t], y_in.at[c, y])

    def d1p(c):
        p_moves[c] = to_planes((c, "p"), lambda t: g_buf.at[c, lo, t], x_buf.at[c, hi, core, lo, y])

    def d1f(c):
        both = toks[c, 1 - hi].reshape(2 * n_tok, feat)
        at = pl.ds(pl.multiple_of(lo * n_rows, n_rows), n_rows)
        rows = jnp.dot(picks[c, at, :], both, preferred_element_type=F32).astype(BF16)
        g_far[c] = rows.reshape(N_Y, ROWS, feat)
        f_moves[c] = to_planes((c, "f"), lambda t: g_far.at[c, t], x_buf.at[c, 1 - hi, core, lo, y])

    def d2(c):
        own_moves[c, "q"].wait()
        received(q_moves[c])
        dst = x_buf.at[c, hi, core, lo]
        x_moves[c] = [remote(y_in.at[c], dst, along_x(1)), remote(y_in.at[c], dst, along_x(3))]

    def d3(c):
        own_moves[c, "p"].wait()
        received(p_moves[c])
        near = x_buf.at[c, hi, core, lo]
        core_moves.setdefault(c, []).append(remote(near, near, partner))
        own_moves[c, "f"].wait()
        received(f_moves[c])
        far = x_buf.at[c, 1 - hi, core, lo]
        core_moves[c].append(remote(far, far, partner))

    def d4(c):
        received(x_moves[c])
        for other in (left, right):
            block = x_buf.at[c, other // N_LO, core, 1 - lo]
            core_moves.setdefault(c, []).append(remote(block, block, partner))

    def d5(c):
        received(core_moves[c])
        sent(core_moves[c])

        def group(g, carry):
            at = pl.ds(pl.multiple_of(g * 2 * CAP, 2 * CAP), 2 * CAP)
            m = N_LO * N_Y * 2 * CAP
            gate = jnp.zeros((m, hidden), F32)
            up = jnp.zeros((m, hidden), F32)
            for q in range(4):
                rows = x_buf[c, q // 2, q % 2, :, :, at, :].reshape(m, feat)
                ks = pl.ds(q * feat, feat)
                gate += jnp.dot(rows, wg[g, ks, :], preferred_element_type=F32)
                up += jnp.dot(rows, wu[g, ks, :], preferred_element_type=F32)
            h = (gate / (1.0 + jnp.exp(-gate)) * up).astype(BF16)
            for q in range(4):
                o = jnp.dot(h, wd[g, :, pl.ds(q * feat, feat)], preferred_element_type=F32)
                x_buf[c, q // 2, q % 2, :, :, at, :] = o.astype(BF16).reshape(
                    N_LO, N_Y, 2 * CAP, feat
                )
            return carry

        lax.fori_loop(0, GROUPS, group, 0)
        reduce_moves[c] = remote(x_buf.at[c, :, 1 - core], core_in.at[c], partner)

    def r1(c):
        received([reduce_moves[c]])

        def add(i, carry):
            h_, s_, y_ = i // (N_LO * N_Y), (i // N_Y) % N_LO, i % N_Y
            total = x_buf[c, h_, core, s_, y_].astype(F32) + core_in[c, h_, s_, y_].astype(F32)
            x_buf[c, h_, core, s_, y_] = total.astype(BF16)
            return carry

        lax.fori_loop(0, N_HI * N_LO * N_Y, add, 0)
        for p, f in enumerate(pieces(c)):
            b_moves[c, p] = [
                remote(
                    x_buf.at[c, other // N_LO, core, par, :, :, f], x_back.at[c, i, :, :, f], along_x(step)
                )
                for i, (other, par, step) in enumerate(
                    ((right, 1 - lo, 1), (left, 1 - lo, 3), (across, lo, 2))
                )
            ]

    def pieces(c):
        if PIECES[c] == 1:
            return [pl.ds(0, feat)]
        cut = (feat // 2 + 127) // 128 * 128
        return [pl.ds(0, cut), pl.ds(cut, feat - cut)]

    def r3(c, p):
        f = pieces(c)[p]
        received(b_moves[c, p])

        def add(i, carry):
            side = x_back[c, 0, i, :, f].astype(F32) + x_back[c, 1, i, :, f].astype(F32)
            y_out[c, 1 - lo, i, :, f] = side.astype(BF16)
            same = x_buf[c, hi, core, lo, i, :, f].astype(F32) + x_back[c, 2, i, :, f].astype(F32)
            y_out[c, lo, i, :, f] = same.astype(BF16)
            return carry

        lax.fori_loop(0, N_Y, add, 0)
        yb_moves[c, p] = [
            remote(y_out.at[c, :, (y + s) % N_Y, :, f], y_back.at[c, :, y, :, f], along_y(s))
            for s in (2, 1, 3)
        ]
        own_back[c, p] = local(y_out.at[c, :, y, :, f], y_back.at[c, :, y, :, f])

    def r4(c, p):
        f = pieces(c)[p]
        own_back[c, p].wait()
        received(yb_moves[c, p])
        rows = y_back[c, :, :, :, f]
        rows = rows.reshape(N_Y * N_LO * ROWS, rows.shape[-1])
        dims = (((0,), (0,)), ((), ()))
        total = lax.dot_general(mix_hi[c], rows, dims, preferred_element_type=F32)
        total = total + lax.dot_general(mix_lo[c], rows, dims, preferred_element_type=F32)
        z_out[c, :, :, f] = total.astype(BF16).reshape(2, n_tok, rows.shape[-1])
        for j, d in enumerate(CHUNKS[c]):
            src, dst = z_out.at[c, j, :, f], z_back.at[c, j, :, f]
            if d:
                zb_moves[c, j, p] = remote(src, dst, along_z(d))
            else:
                own_z.append(local(src, dst))

    own_z, own_back = [], {}

    def own():
        for load in own_loads:
            load.wait()

    def load_weights():
        for load in weight_loads:
            load.wait()
        f = planned_of(expert)

        def pick_rows(i, carry):
            at = pl.ds(pl.multiple_of(i * 128, 128), 128)
            for w in (wg, wu):
                w[2, at, :] = (w[0, at, :].astype(F32) * (1.0 - f) + w[1, at, :].astype(F32) * f).astype(BF16)
            return carry

        lax.fori_loop(0, wg.shape[1] // 128, pick_rows, 0)

        def pick_down(i, carry):
            at = pl.ds(pl.multiple_of(i * 16, 16), 16)
            wd[2, at, :] = (wd[0, at, :].astype(F32) * (1.0 - f) + wd[1, at, :].astype(F32) * f).astype(BF16)
            return carry

        lax.fori_loop(0, hidden // 16, pick_down, 0)

    swap()
    z_near(0)
    z_near(1)
    z_near(-1)
    d1(0)
    z_far(0)
    load_weights()
    d2(0)
    d1p(0)
    z_near(2)
    z_near(-2)
    d1(1)
    z_far(1)
    z_far(-1)
    d1f(0)
    d2(1)
    d1p(1)
    d4(0)
    d3(0)
    z_near(3)
    z_near(-3)
    z_far(2)
    z_far(-2)
    d1(2)
    d1f(1)
    d5(0)
    d2(2)
    d1p(2)
    r1(0)
    z_near(4)
    own()
    d1(3)
    z_far(3)
    z_far(-3)
    d1f(2)
    d3(1)
    d4(1)
    d5(1)
    d2(3)
    d1p(3)
    r1(1)
    z_far(4)
    d1f(3)
    d3(2)
    d4(2)
    r3(0, 0)
    d5(2)
    r4(0, 0)
    r1(2)
    d3(3)
    d4(3)
    d5(3)
    r3(1, 0)
    r1(3)
    r4(1, 0)
    r3(2, 0)
    r4(2, 0)
    r3(3, 0)
    r4(3, 0)
    r3(3, 1)
    r4(3, 1)
    for copy in own_z:
        copy.wait()
    received(zb_moves.values())

    def finish(i, carry):
        at = pl.ds(pl.multiple_of(i * 16, 16), 16)
        total = jnp.zeros((16, feat), F32)
        for c in range(n_chunk):
            for j in range(2):
                total = total + z_back[c, j, at, :].astype(F32)
        out_ref[at, :] = total.astype(out_ref.dtype)
        return carry

    lax.fori_loop(0, n_tok // 16, finish, 0)
    sent(list(started))


N_REMOTE = 22 + 4 * (9 + 2 + 4 + 1) + 5 * (3 + 3) + 8
N_LOCAL = 4 + 4 * 3 + 5 + 2


def per_device(tokens, expert_ids, gate_weights, replica_plan, w_gate, w_up, w_down):
    owners = lax.axis_size("expert")
    n_z = owners // (N_LO * N_Y)
    tok, feat = tokens.shape
    width = w_gate.shape[1]
    hidden = w_gate.shape[2]
    n_chunk = len(CHUNKS)
    vmem = pl.BlockSpec(memory_space=pltpu.VMEM)
    hbm = pl.BlockSpec(memory_space=pl.ANY)
    block = (N_Y, ROWS, feat)
    slot_rows = N_Y * N_LO * ROWS
    return pl.pallas_call(
        functools.partial(kernel, n_z),
        out_shape=jax.ShapeDtypeStruct((tok, feat), BF16),
        in_specs=[vmem, vmem, vmem, pl.BlockSpec(memory_space=pltpu.SMEM), hbm, hbm, hbm],
        out_specs=vmem,
        scratch_shapes=[
            pltpu.VMEM((3, width, hidden), BF16),
            pltpu.VMEM((3, width, hidden), BF16),
            pltpu.VMEM((3, hidden, width), BF16),
            pltpu.VMEM((n_chunk, N_HI, 2, tok, feat), BF16),
            pltpu.VMEM((n_chunk, 2, 16, tok), F32),
            pltpu.VMEM((16, tok), F32),
            pltpu.VMEM((n_chunk, slot_rows, 2 * tok), BF16),
            pltpu.VMEM((n_chunk, slot_rows, 2 * tok), BF16),
            pltpu.VMEM((n_chunk, slot_rows, 2 * tok), BF16),
            pltpu.VMEM((n_chunk, N_LO) + block, BF16),
            pltpu.VMEM((n_chunk,) + block, BF16),
            pltpu.VMEM((n_chunk,) + block, BF16),
            pltpu.VMEM((n_chunk, N_HI, N_CORE, N_LO) + block, BF16),
            pltpu.VMEM((n_chunk, N_HI, N_LO) + block, BF16),
            pltpu.VMEM((n_chunk, 3) + block, BF16),
            pltpu.VMEM((n_chunk, N_LO) + block, BF16),
            pltpu.VMEM((n_chunk, N_LO) + block, BF16),
            pltpu.VMEM((n_chunk, 2, tok, feat), BF16),
            pltpu.VMEM((n_chunk, 2, tok, feat), BF16),
            pltpu.SemaphoreType.DMA((N_REMOTE,)),
            pltpu.SemaphoreType.DMA((N_REMOTE,)),
            pltpu.SemaphoreType.DMA((N_LOCAL,)),
        ],
        compiler_params=pltpu.CompilerParams(
            collective_id=0, has_side_effects=True, vmem_limit_bytes=67043328
        ),
    )(tokens, expert_ids.T, gate_weights.T, replica_plan, w_gate, w_up, w_down)


def solution(mesh):
    in_specs = (
        P("expert", "dp"),
        P("expert", None),
        P("expert", None),
        P(),
        P("expert", None, "dp"),
        P("expert", None, "dp"),
        P("expert", "dp", None),
    )
    return jax.shard_map(
        per_device, mesh=mesh, in_specs=in_specs, out_specs=P("expert", "dp"), check_vma=False
    )
```

```python
import functools

import jax
import jax.numpy as jnp
from jax import lax
from jax.experimental import pallas as pl
from jax.experimental.pallas import tpu as pltpu
from jax.sharding import PartitionSpec as P

CAP = 8
N_LO, N_Y, N_HI, N_CORE = 2, 4, 2, 2
N_X = N_LO * N_HI
GROUPS = 3
ROWS = GROUPS * 2 * CAP
CHUNKS = ((1, -1), (2, -2), (3, -3), (0, 4))
PIECES = (2, 3, 2, 2)
BF16, F32 = jnp.bfloat16, jnp.float32


def kernel(
    n_z, tok_ref, ids_ref, gate_ref, plan_ref, wg_hbm, wu_hbm, wd_hbm, out_ref,
    wg, wu, wd, toks, metas, meta_own, picks, mix_hi, mix_lo, g_buf, g_far, y_in, x_buf, core_in,
    x_back, y_out, y_back, z_out, z_back,
    send_sem, recv_sem, local_sem,
):
    expert = lax.axis_index("expert")
    dp = lax.axis_index("dp")
    z, lo, y = expert // (N_LO * N_Y), (expert // N_Y) % N_LO, expert % N_Y
    hi, core = dp // N_CORE, dp % N_CORE
    x = hi * N_LO + lo
    n_tok = tok_ref.shape[0]
    feat = tok_ref.shape[1]
    hidden = wg.shape[2]
    n_chunk = len(CHUNKS)

    def device(z_, x_, y_, core_):
        return ((z_ * N_LO + x_ % N_LO) * N_Y + y_, (x_ // N_LO) * N_CORE + core_)

    def along_z(step):
        return device((z + step + n_z) % n_z, x, y, core)

    def along_y(step):
        return device(z, x, (y + step) % N_Y, core)

    def along_x(step):
        return device(z, (x + step) % N_X, y, core)

    right, left = (x + 1) % N_X, (x + N_X - 1) % N_X
    across = (x + 2) % N_X
    partner = device(z, x, y, 1 - core)

    started = []
    count = [0]
    local_count = [0]

    def remote(src, dst, target):
        i = count[0]
        count[0] += 1
        copy = pltpu.make_async_remote_copy(
            src_ref=src, dst_ref=dst, send_sem=send_sem.at[i], recv_sem=recv_sem.at[i],
            device_id=target, device_id_type=pl.DeviceIdType.MESH,
        )
        copy.start()
        started.append(copy)
        return copy

    def local(src, dst):
        i = local_count[0]
        local_count[0] += 1
        copy = pltpu.make_async_copy(src, dst, local_sem.at[i])
        copy.start()
        return copy

    def received(copies):
        for c in copies:
            c.wait_recv()

    def sent(copies):
        for c in copies:
            c.wait_send()
            started[:] = [other for other in started if other is not c]

    weight_loads = [
        local(wg_hbm, wg.at[pl.ds(0, 2)]),
        local(wu_hbm, wu.at[pl.ds(0, 2)]),
        local(wd_hbm, wd.at[pl.ds(0, 2)]),
    ]
    where = {d: (c, j) for c, pair in enumerate(CHUNKS) for j, d in enumerate(pair)}

    def tok_at(d, h):
        c, j = where[d]
        return toks.at[c, h, j]

    own_loads = [local(tok_ref, tok_at(0, hi))]
    meta_own[pl.ds(0, 8), :] = ids_ref[...].astype(F32)
    meta_own[pl.ds(8, 8), :] = gate_ref[...]
    metas[where[0]] = meta_own[...]

    barrier = pltpu.get_barrier_semaphore()
    peers = [along_z(s) for s in range(1, n_z)] + [along_y(s) for s in range(1, N_Y)]
    peers += [along_x(1), along_x(2), along_x(3), partner]
    for peer in peers:
        pl.semaphore_signal(barrier, inc=1, device_id=peer, device_id_type=pl.DeviceIdType.MESH)
    pl.semaphore_wait(barrier, len(peers))

    z_in, z_meta = {}, {}

    def z_near(d):
        for s in ((1, -1) if d == 0 else (1,) if d > 0 else (-1,)):
            if d:
                received([z_in[d, 0], z_meta[d]])
            nxt = d + s
            if nxt in where:
                src = tok_at(d, hi) if d else tok_ref
                src_m = metas.at[where[d]] if d else meta_own
                z_in[nxt, 0] = remote(src, tok_at(nxt, hi), along_z(-s))
                z_meta[nxt] = remote(src_m, metas.at[where[nxt]], along_z(-s))

    def z_far(d):
        received([z_in[d, 1]])
        for s in ((1, -1) if d == 0 else (1,) if d > 0 else (-1,)):
            nxt = d + s
            if nxt in where:
                z_in[nxt, 1] = remote(tok_at(d, 1 - hi), tok_at(nxt, 1 - hi), along_z(-s))

    def swap():
        z_in[0, 1] = remote(tok_ref, tok_at(0, hi), along_x(2))

    before = (
        lax.broadcasted_iota(jnp.int32, (n_tok, n_tok), 0)
        < lax.broadcasted_iota(jnp.int32, (n_tok, n_tok), 1)
    ).astype(F32).astype(BF16)
    plane = N_LO * N_Y
    place = lax.broadcasted_iota(jnp.int32, (CAP, n_tok), 0).astype(F32)
    blank = jnp.zeros((CAP, n_tok), F32)

    def planned_of(owner):
        owners = n_z * plane
        return (plan_ref[(owner + owners // 2) % owners] - 2 * owner).astype(F32)

    def slots(c):
        keys, gates = [], []
        ids = lax.broadcasted_iota(jnp.int32, (2 * plane, n_tok), 0) + z * (2 * plane)
        ids = ids.astype(F32)
        for j in range(2):
            meta = metas[c, j]
            member = jnp.zeros((2 * plane, n_tok), F32)
            gate = jnp.zeros((2 * plane, n_tok), F32)
            for k in range(8):
                hit = meta[k : k + 1, :] == ids
                member = jnp.where(hit, 1.0, member)
                gate = jnp.where(hit, meta[8 + k : 9 + k, :], gate)
            rank = jnp.dot(member.astype(BF16), before, preferred_element_type=F32)
            keys.append(jnp.where(member > 0.5, rank, -1.0))
            gates.append(gate)
        for yy in range(N_Y):
            for ll in range(N_LO):
                r = ll * (2 * N_Y) + yy * 2
                f = planned_of(z * plane + ll * N_Y + yy)
                base = (ll * N_Y + yy) * ROWS
                for g in range(GROUPS):
                    ones, weights = [], []
                    for j in range(2):
                        k0, k1 = keys[j][r : r + 1, :], keys[j][r + 1 : r + 2, :]
                        w0, w1 = gates[j][r : r + 1, :], gates[j][r + 1 : r + 2, :]
                        if g == 0:
                            k, w = k0, w0
                        elif g == 1:
                            k, w = k1, w1
                        else:
                            k = k0 * (1.0 - f) + k1 * f - float(CAP)
                            w = w0 * (1.0 - f) + w1 * f
                        hit = jnp.broadcast_to(k, (CAP, n_tok)) == place
                        one = jnp.where(hit, 1.0, 0.0)
                        weight = jnp.where(hit, jnp.broadcast_to(w, (CAP, n_tok)), 0.0)
                        row1 = [blank, blank]
                        row2 = [blank, blank]
                        row1[j], row2[j] = one, weight
                        ones.append(jnp.concatenate(row1, axis=1))
                        weights.append(jnp.concatenate(row2, axis=1))
                    at = pl.ds(base + g * 2 * CAP, 2 * CAP)
                    picks[c, at, :] = jnp.concatenate(ones, axis=0).astype(BF16)
                    w = jnp.concatenate(weights, axis=0)
                    high = w.astype(BF16)
                    mix_hi[c, at, :] = high
                    mix_lo[c, at, :] = (w - high.astype(F32)).astype(BF16)

    q_moves, p_moves, f_moves, x_moves, core_moves, own_moves = {}, {}, {}, {}, {}, {}
    reduce_moves, b_moves, yb_moves, zb_moves = {}, {}, {}, {}
    n_rows = N_Y * ROWS

    def to_planes(key, src, dst):
        moves = [remote(src((y + s) % N_Y), dst, along_y(s)) for s in (2, 1, 3)]
        own_moves[key] = local(src(y), dst)
        return moves

    def d1(c):
        slots(c)
        both = toks[c, hi].reshape(2 * n_tok, feat)
        rows = jnp.dot(picks[c], both, preferred_element_type=F32).astype(BF16)
        g_buf[c] = rows.reshape(N_LO, N_Y, ROWS, feat)
        q_moves[c] = to_planes((c, "q"), lambda t: g_buf.at[c, 1 - lo, t], y_in.at[c, y])

    def d1p(c):
        p_moves[c] = to_planes((c, "p"), lambda t: g_buf.at[c, lo, t], x_buf.at[c, hi, core, lo, y])

    def d1f(c):
        both = toks[c, 1 - hi].reshape(2 * n_tok, feat)
        at = pl.ds(pl.multiple_of(lo * n_rows, n_rows), n_rows)
        rows = jnp.dot(picks[c, at, :], both, preferred_element_type=F32).astype(BF16)
        g_far[c] = rows.reshape(N_Y, ROWS, feat)
        f_moves[c] = to_planes((c, "f"), lambda t: g_far.at[c, t], x_buf.at[c, 1 - hi, core, lo, y])

    def d2(c):
        own_moves[c, "q"].wait()
        received(q_moves[c])
        dst = x_buf.at[c, hi, core, lo]
        x_moves[c] = [remote(y_in.at[c], dst, along_x(1)), remote(y_in.at[c], dst, along_x(3))]

    def d3(c):
        own_moves[c, "p"].wait()
        received(p_moves[c])
        near = x_buf.at[c, hi, core, lo]
        core_moves.setdefault(c, []).append(remote(near, near, partner))
        own_moves[c, "f"].wait()
        received(f_moves[c])
        far = x_buf.at[c, 1 - hi, core, lo]
        core_moves[c].append(remote(far, far, partner))

    def d4(c):
        received(x_moves[c])
        for other in (left, right):
            block = x_buf.at[c, other // N_LO, core, 1 - lo]
            core_moves.setdefault(c, []).append(remote(block, block, partner))

    def d5(c):
        received(core_moves[c])
        sent(core_moves[c])

        def group(g, carry):
            at = pl.ds(pl.multiple_of(g * 2 * CAP, 2 * CAP), 2 * CAP)
            m = N_LO * N_Y * 2 * CAP
            gate = jnp.zeros((m, hidden), F32)
            up = jnp.zeros((m, hidden), F32)
            for q in range(4):
                rows = x_buf[c, q // 2, q % 2, :, :, at, :].reshape(m, feat)
                ks = pl.ds(q * feat, feat)
                gate += jnp.dot(rows, wg[g, ks, :], preferred_element_type=F32)
                up += jnp.dot(rows, wu[g, ks, :], preferred_element_type=F32)
            h = (gate / (1.0 + jnp.exp(-gate)) * up).astype(BF16)
            for q in range(4):
                o = jnp.dot(h, wd[g, :, pl.ds(q * feat, feat)], preferred_element_type=F32)
                x_buf[c, q // 2, q % 2, :, :, at, :] = o.astype(BF16).reshape(
                    N_LO, N_Y, 2 * CAP, feat
                )
            return carry

        lax.fori_loop(0, GROUPS, group, 0)
        reduce_moves[c] = remote(x_buf.at[c, :, 1 - core], core_in.at[c], partner)

    def r1(c):
        received([reduce_moves[c]])

        def add(i, carry):
            h_, s_, y_ = i // (N_LO * N_Y), (i // N_Y) % N_LO, i % N_Y
            total = x_buf[c, h_, core, s_, y_].astype(F32) + core_in[c, h_, s_, y_].astype(F32)
            x_buf[c, h_, core, s_, y_] = total.astype(BF16)
            return carry

        lax.fori_loop(0, N_HI * N_LO * N_Y, add, 0)
        for p, f in enumerate(pieces(c)):
            b_moves[c, p] = [
                remote(
                    x_buf.at[c, other // N_LO, core, par, :, :, f], x_back.at[c, i, :, :, f], along_x(step)
                )
                for i, (other, par, step) in enumerate(
                    ((right, 1 - lo, 1), (left, 1 - lo, 3), (across, lo, 2))
                )
            ]

    def pieces(c):
        tiles = feat // 128
        ends = [-(-tiles * (i + 1) // PIECES[c]) for i in range(PIECES[c])]
        starts = [0] + ends[:-1]
        return [pl.ds(128 * i, 128 * (j - i)) for i, j in zip(starts, ends)]

    def r3(c, p):
        f = pieces(c)[p]
        received(b_moves[c, p])

        def add(i, carry):
            side = x_back[c, 0, i, :, f].astype(F32) + x_back[c, 1, i, :, f].astype(F32)
            y_out[c, 1 - lo, i, :, f] = side.astype(BF16)
            same = x_buf[c, hi, core, lo, i, :, f].astype(F32) + x_back[c, 2, i, :, f].astype(F32)
            y_out[c, lo, i, :, f] = same.astype(BF16)
            return carry

        lax.fori_loop(0, N_Y, add, 0)
        yb_moves[c, p] = [
            remote(y_out.at[c, :, (y + s) % N_Y, :, f], y_back.at[c, :, y, :, f], along_y(s))
            for s in (2, 1, 3)
        ]
        own_back[c, p] = local(y_out.at[c, :, y, :, f], y_back.at[c, :, y, :, f])

    def r4(c, p):
        f = pieces(c)[p]
        own_back[c, p].wait()
        received(yb_moves[c, p])
        rows = y_back[c, :, :, :, f]
        rows = rows.reshape(N_Y * N_LO * ROWS, rows.shape[-1])
        dims = (((0,), (0,)), ((), ()))
        total = lax.dot_general(mix_hi[c], rows, dims, preferred_element_type=F32)
        total = total + lax.dot_general(mix_lo[c], rows, dims, preferred_element_type=F32)
        z_out[c, :, :, f] = total.astype(BF16).reshape(2, n_tok, rows.shape[-1])
        for j, d in enumerate(CHUNKS[c]):
            src, dst = z_out.at[c, j, :, f], z_back.at[c, j, :, f]
            if d:
                zb_moves[c, j, p] = remote(src, dst, along_z(d))
            else:
                own_z.append(local(src, dst))

    own_z, own_back = [], {}

    def own():
        for load in own_loads:
            load.wait()

    def load_weights():
        for load in weight_loads:
            load.wait()
        f = planned_of(expert)

        def pick_rows(i, carry):
            at = pl.ds(pl.multiple_of(i * 128, 128), 128)
            for w in (wg, wu):
                w[2, at, :] = (w[0, at, :].astype(F32) * (1.0 - f) + w[1, at, :].astype(F32) * f).astype(BF16)
            return carry

        lax.fori_loop(0, wg.shape[1] // 128, pick_rows, 0)

        def pick_down(i, carry):
            at = pl.ds(pl.multiple_of(i * 16, 16), 16)
            wd[2, at, :] = (wd[0, at, :].astype(F32) * (1.0 - f) + wd[1, at, :].astype(F32) * f).astype(BF16)
            return carry

        lax.fori_loop(0, hidden // 16, pick_down, 0)

    z_near(0)
    swap()
    z_near(1)
    z_near(-1)
    d1(0)
    z_near(-2)
    z_near(2)
    d1(1)
    d1p(0)
    d2(0)
    load_weights()
    z_far(0)
    own()
    z_near(3)
    d2(1)
    z_near(-3)
    d1(2)
    z_far(-1)
    z_far(1)
    d1f(0)
    d2(2)
    z_near(4)
    d1(3)
    d3(0)
    d4(0)
    z_far(-2)
    d1p(2)
    z_far(2)
    d2(3)
    d5(0)
    z_far(-3)
    z_far(3)
    d1f(2)
    d4(1)
    d1p(3)
    r1(0)
    d4(3)
    d4(2)
    d3(2)
    z_far(4)
    d1f(3)
    d1f(1)
    d5(2)
    d1p(1)
    r3(0, 0)
    r1(2)
    d3(3)
    r3(0, 1)
    d5(3)
    r4(0, 1)
    r3(2, 0)
    d3(1)
    r4(0, 0)
    r1(3)
    d5(1)
    r3(2, 1)
    r4(2, 0)
    r4(2, 1)
    r1(1)
    r3(3, 0)
    r3(3, 1)
    r4(3, 0)
    r4(3, 1)
    r3(1, 0)
    r3(1, 1)
    r4(1, 0)
    r3(1, 2)
    r4(1, 1)
    r4(1, 2)
    for copy in own_z:
        copy.wait()
    received(zb_moves.values())

    def finish(i, carry):
        at = pl.ds(pl.multiple_of(i * 16, 16), 16)
        total = jnp.zeros((16, feat), F32)
        for c in range(n_chunk):
            for j in range(2):
                total = total + z_back[c, j, at, :].astype(F32)
        out_ref[at, :] = total.astype(out_ref.dtype)
        return carry

    lax.fori_loop(0, n_tok // 16, finish, 0)
    sent(list(started))


N_REMOTE = 22 + 4 * (9 + 2 + 4 + 1) + sum(
    n * (6 + sum(d != 0 for d in pair)) for n, pair in zip(PIECES, CHUNKS)
)
N_LOCAL = 4 + 4 * 3 + sum(n * (1 + (0 in pair)) for n, pair in zip(PIECES, CHUNKS))


def per_device(tokens, expert_ids, gate_weights, replica_plan, w_gate, w_up, w_down):
    owners = lax.axis_size("expert")
    n_z = owners // (N_LO * N_Y)
    tok, feat = tokens.shape
    width = w_gate.shape[1]
    hidden = w_gate.shape[2]
    n_chunk = len(CHUNKS)
    vmem = pl.BlockSpec(memory_space=pltpu.VMEM)
    hbm = pl.BlockSpec(memory_space=pl.ANY)
    block = (N_Y, ROWS, feat)
    slot_rows = N_Y * N_LO * ROWS
    return pl.pallas_call(
        functools.partial(kernel, n_z),
        out_shape=jax.ShapeDtypeStruct((tok, feat), BF16),
        in_specs=[vmem, vmem, vmem, pl.BlockSpec(memory_space=pltpu.SMEM), hbm, hbm, hbm],
        out_specs=vmem,
        scratch_shapes=[
            pltpu.VMEM((3, width, hidden), BF16),
            pltpu.VMEM((3, width, hidden), BF16),
            pltpu.VMEM((3, hidden, width), BF16),
            pltpu.VMEM((n_chunk, N_HI, 2, tok, feat), BF16),
            pltpu.VMEM((n_chunk, 2, 16, tok), F32),
            pltpu.VMEM((16, tok), F32),
            pltpu.VMEM((n_chunk, slot_rows, 2 * tok), BF16),
            pltpu.VMEM((n_chunk, slot_rows, 2 * tok), BF16),
            pltpu.VMEM((n_chunk, slot_rows, 2 * tok), BF16),
            pltpu.VMEM((n_chunk, N_LO) + block, BF16),
            pltpu.VMEM((n_chunk,) + block, BF16),
            pltpu.VMEM((n_chunk,) + block, BF16),
            pltpu.VMEM((n_chunk, N_HI, N_CORE, N_LO) + block, BF16),
            pltpu.VMEM((n_chunk, N_HI, N_LO) + block, BF16),
            pltpu.VMEM((n_chunk, 3) + block, BF16),
            pltpu.VMEM((n_chunk, N_LO) + block, BF16),
            pltpu.VMEM((n_chunk, N_LO) + block, BF16),
            pltpu.VMEM((n_chunk, 2, tok, feat), BF16),
            pltpu.VMEM((n_chunk, 2, tok, feat), BF16),
            pltpu.SemaphoreType.DMA((N_REMOTE,)),
            pltpu.SemaphoreType.DMA((N_REMOTE,)),
            pltpu.SemaphoreType.DMA((N_LOCAL,)),
        ],
        compiler_params=pltpu.CompilerParams(
            collective_id=0, has_side_effects=True, vmem_limit_bytes=67043328
        ),
    )(tokens, expert_ids.T, gate_weights.T, replica_plan, w_gate, w_up, w_down)


def solution(mesh):
    in_specs = (
        P("expert", "dp"),
        P("expert", None),
        P("expert", None),
        P(),
        P("expert", None, "dp"),
        P("expert", None, "dp"),
        P("expert", "dp", None),
    )
    return jax.shard_map(
        per_device, mesh=mesh, in_specs=in_specs, out_specs=P("expert", "dp"), check_vma=False
    )
```

```python
import functools

import jax
import jax.numpy as jnp
from jax import lax
from jax.experimental import pallas as pl
from jax.experimental.pallas import tpu as pltpu
from jax.sharding import PartitionSpec as P

CAP = 8
N_LO, N_Y, N_HI, N_CORE = 2, 4, 2, 2
N_X = N_LO * N_HI
GROUPS = 3
ROWS = GROUPS * 2 * CAP
CHUNKS = ((1, -1), (2, -2), (3, -3), (0, 4))
PIECES = (2, 3, 2, 2)
DIRECT = (0,)
MERGE = ()
BF16, F32 = jnp.bfloat16, jnp.float32


def kernel(
    n_z, tok_ref, ids_ref, gate_ref, plan_ref, wg_hbm, wu_hbm, wd_hbm, out_ref,
    wg, wu, wd, toks, metas, meta_own, picks, mix_hi, mix_lo, g_buf, g_far, y_in, x_buf, core_in,
    x_back, y_out, y_back, z_out, z_back, far_back, far_out, far_in, merged, swap_out, swap_in,
    send_sem, recv_sem, local_sem,
):
    expert = lax.axis_index("expert")
    dp = lax.axis_index("dp")
    z, lo, y = expert // (N_LO * N_Y), (expert // N_Y) % N_LO, expert % N_Y
    hi, core = dp // N_CORE, dp % N_CORE
    x = hi * N_LO + lo
    n_tok = tok_ref.shape[0]
    feat = tok_ref.shape[1]
    hidden = wg.shape[2]
    n_chunk = len(CHUNKS)

    def device(z_, x_, y_, core_):
        return ((z_ * N_LO + x_ % N_LO) * N_Y + y_, (x_ // N_LO) * N_CORE + core_)

    def along_z(step):
        return device((z + step + n_z) % n_z, x, y, core)

    def along_y(step):
        return device(z, x, (y + step) % N_Y, core)

    def along_x(step):
        return device(z, (x + step) % N_X, y, core)

    right, left = (x + 1) % N_X, (x + N_X - 1) % N_X
    across = (x + 2) % N_X
    partner = device(z, x, y, 1 - core)

    started = []
    count = [0]
    local_count = [0]

    def remote(src, dst, target):
        i = count[0]
        count[0] += 1
        copy = pltpu.make_async_remote_copy(
            src_ref=src, dst_ref=dst, send_sem=send_sem.at[i], recv_sem=recv_sem.at[i],
            device_id=target, device_id_type=pl.DeviceIdType.MESH,
        )
        copy.start()
        started.append(copy)
        return copy

    def local(src, dst):
        i = local_count[0]
        local_count[0] += 1
        copy = pltpu.make_async_copy(src, dst, local_sem.at[i])
        copy.start()
        return copy

    def received(copies):
        for c in copies:
            c.wait_recv()

    def sent(copies):
        for c in copies:
            c.wait_send()
            started[:] = [other for other in started if other is not c]

    weight_loads = [
        local(wg_hbm, wg.at[pl.ds(0, 2)]),
        local(wu_hbm, wu.at[pl.ds(0, 2)]),
        local(wd_hbm, wd.at[pl.ds(0, 2)]),
    ]
    where = {d: (c, j) for c, pair in enumerate(CHUNKS) for j, d in enumerate(pair)}

    def tok_at(d, h):
        c, j = where[d]
        return toks.at[c, h, j]

    own_loads = [local(tok_ref, tok_at(0, hi))]
    meta_own[pl.ds(0, 8), :] = ids_ref[...].astype(F32)
    meta_own[pl.ds(8, 8), :] = gate_ref[...]
    metas[where[0]] = meta_own[...]

    barrier = pltpu.get_barrier_semaphore()
    peers = [along_z(s) for s in range(1, n_z)] + [along_y(s) for s in range(1, N_Y)]
    peers += [along_x(1), along_x(2), along_x(3), partner]
    for peer in peers:
        pl.semaphore_signal(barrier, inc=1, device_id=peer, device_id_type=pl.DeviceIdType.MESH)
    pl.semaphore_wait(barrier, len(peers))

    z_in, z_meta = {}, {}

    def z_near(d):
        for s in ((1, -1) if d == 0 else (1,) if d > 0 else (-1,)):
            if d:
                received([z_in[d, 0], z_meta[d]])
            nxt = d + s
            if nxt in where:
                src = tok_at(d, hi) if d else tok_ref
                src_m = metas.at[where[d]] if d else meta_own
                z_in[nxt, 0] = remote(src, tok_at(nxt, hi), along_z(-s))
                z_meta[nxt] = remote(src_m, metas.at[where[nxt]], along_z(-s))

    def z_far(d):
        received([z_in[d, 1]])
        for s in ((1, -1) if d == 0 else (1,) if d > 0 else (-1,)):
            nxt = d + s
            if nxt in where:
                z_in[nxt, 1] = remote(tok_at(d, 1 - hi), tok_at(nxt, 1 - hi), along_z(-s))

    def swap():
        z_in[0, 1] = remote(tok_ref, tok_at(0, hi), along_x(2))

    before = (
        lax.broadcasted_iota(jnp.int32, (n_tok, n_tok), 0)
        < lax.broadcasted_iota(jnp.int32, (n_tok, n_tok), 1)
    ).astype(F32).astype(BF16)
    plane = N_LO * N_Y
    place = lax.broadcasted_iota(jnp.int32, (CAP, n_tok), 0).astype(F32)
    blank = jnp.zeros((CAP, n_tok), F32)

    def planned_of(owner):
        owners = n_z * plane
        return (plan_ref[(owner + owners // 2) % owners] - 2 * owner).astype(F32)

    def slots(c):
        keys, gates = [], []
        ids = lax.broadcasted_iota(jnp.int32, (2 * plane, n_tok), 0) + z * (2 * plane)
        ids = ids.astype(F32)
        for j in range(2):
            meta = metas[c, j]
            member = jnp.zeros((2 * plane, n_tok), F32)
            gate = jnp.zeros((2 * plane, n_tok), F32)
            for k in range(8):
                hit = meta[k : k + 1, :] == ids
                member = jnp.where(hit, 1.0, member)
                gate = jnp.where(hit, meta[8 + k : 9 + k, :], gate)
            rank = jnp.dot(member.astype(BF16), before, preferred_element_type=F32)
            keys.append(jnp.where(member > 0.5, rank, -1.0))
            gates.append(gate)
        for yy in range(N_Y):
            for ll in range(N_LO):
                r = ll * (2 * N_Y) + yy * 2
                f = planned_of(z * plane + ll * N_Y + yy)
                base = (ll * N_Y + yy) * ROWS
                for g in range(GROUPS):
                    ones, weights = [], []
                    for j in range(2):
                        k0, k1 = keys[j][r : r + 1, :], keys[j][r + 1 : r + 2, :]
                        w0, w1 = gates[j][r : r + 1, :], gates[j][r + 1 : r + 2, :]
                        if g == 0:
                            k, w = k0, w0
                        elif g == 1:
                            k, w = k1, w1
                        else:
                            k = k0 * (1.0 - f) + k1 * f - float(CAP)
                            w = w0 * (1.0 - f) + w1 * f
                        hit = jnp.broadcast_to(k, (CAP, n_tok)) == place
                        one = jnp.where(hit, 1.0, 0.0)
                        weight = jnp.where(hit, jnp.broadcast_to(w, (CAP, n_tok)), 0.0)
                        row1 = [blank, blank]
                        row2 = [blank, blank]
                        row1[j], row2[j] = one, weight
                        ones.append(jnp.concatenate(row1, axis=1))
                        weights.append(jnp.concatenate(row2, axis=1))
                    at = pl.ds(base + g * 2 * CAP, 2 * CAP)
                    picks[c, at, :] = jnp.concatenate(ones, axis=0).astype(BF16)
                    w = jnp.concatenate(weights, axis=0)
                    high = w.astype(BF16)
                    mix_hi[c, at, :] = high
                    mix_lo[c, at, :] = (w - high.astype(F32)).astype(BF16)

    q_moves, p_moves, f_moves, x_moves, core_moves, own_moves = {}, {}, {}, {}, {}, {}
    reduce_moves, b_moves, yb_moves, zb_moves = {}, {}, {}, {}
    n_rows = N_Y * ROWS

    def to_planes(key, src, dst):
        moves = [remote(src((y + s) % N_Y), dst, along_y(s)) for s in (2, 1, 3)]
        own_moves[key] = local(src(y), dst)
        return moves

    def d1(c):
        slots(c)
        both = toks[c, hi].reshape(2 * n_tok, feat)
        rows = jnp.dot(picks[c], both, preferred_element_type=F32).astype(BF16)
        g_buf[c] = rows.reshape(N_LO, N_Y, ROWS, feat)
        q_moves[c] = to_planes((c, "q"), lambda t: g_buf.at[c, 1 - lo, t], y_in.at[c, y])

    def d1p(c):
        p_moves[c] = to_planes((c, "p"), lambda t: g_buf.at[c, lo, t], x_buf.at[c, hi, core, lo, y])

    def d1f(c):
        both = toks[c, 1 - hi].reshape(2 * n_tok, feat)
        at = pl.ds(pl.multiple_of(lo * n_rows, n_rows), n_rows)
        rows = jnp.dot(picks[c, at, :], both, preferred_element_type=F32).astype(BF16)
        g_far[c] = rows.reshape(N_Y, ROWS, feat)
        f_moves[c] = to_planes((c, "f"), lambda t: g_far.at[c, t], x_buf.at[c, 1 - hi, core, lo, y])

    def d2(c):
        own_moves[c, "q"].wait()
        received(q_moves[c])
        dst = x_buf.at[c, hi, core, lo]
        x_moves[c] = [remote(y_in.at[c], dst, along_x(1)), remote(y_in.at[c], dst, along_x(3))]

    def d3(c):
        own_moves[c, "p"].wait()
        received(p_moves[c])
        near = x_buf.at[c, hi, core, lo]
        core_moves.setdefault(c, []).append(remote(near, near, partner))
        own_moves[c, "f"].wait()
        received(f_moves[c])
        far = x_buf.at[c, 1 - hi, core, lo]
        core_moves[c].append(remote(far, far, partner))

    def d4(c):
        received(x_moves[c])
        for other in (left, right):
            block = x_buf.at[c, other // N_LO, core, 1 - lo]
            core_moves.setdefault(c, []).append(remote(block, block, partner))

    def d5(c):
        received(core_moves[c])
        sent(core_moves[c])

        def group(g, carry):
            at = pl.ds(pl.multiple_of(g * 2 * CAP, 2 * CAP), 2 * CAP)
            m = N_LO * N_Y * 2 * CAP
            gate = jnp.zeros((m, hidden), F32)
            up = jnp.zeros((m, hidden), F32)
            for q in range(4):
                rows = x_buf[c, q // 2, q % 2, :, :, at, :].reshape(m, feat)
                ks = pl.ds(q * feat, feat)
                gate += jnp.dot(rows, wg[g, ks, :], preferred_element_type=F32)
                up += jnp.dot(rows, wu[g, ks, :], preferred_element_type=F32)
            h = (gate / (1.0 + jnp.exp(-gate)) * up).astype(BF16)
            for q in range(4):
                o = jnp.dot(h, wd[g, :, pl.ds(q * feat, feat)], preferred_element_type=F32)
                x_buf[c, q // 2, q % 2, :, :, at, :] = o.astype(BF16).reshape(
                    N_LO, N_Y, 2 * CAP, feat
                )
            return carry

        lax.fori_loop(0, GROUPS, group, 0)
        reduce_moves[c] = remote(x_buf.at[c, :, 1 - core], core_in.at[c], partner)

    def r1(c):
        received([reduce_moves[c]])

        def add(i, carry):
            h_, s_, y_ = i // (N_LO * N_Y), (i // N_Y) % N_LO, i % N_Y
            total = x_buf[c, h_, core, s_, y_].astype(F32) + core_in[c, h_, s_, y_].astype(F32)
            x_buf[c, h_, core, s_, y_] = total.astype(BF16)
            return carry

        lax.fori_loop(0, N_HI * N_LO * N_Y, add, 0)
        for p, f in enumerate(pieces(c)):
            b_moves[c, p] = [
                remote(
                    x_buf.at[c, other // N_LO, core, par, :, :, f], x_back.at[c, i, :, :, f], along_x(step)
                )
                for i, (other, par, step) in enumerate(
                    ((right, 1 - lo, 1), (left, 1 - lo, 3), (across, lo, 2))[: 2 if c in DIRECT else 3]
                )
            ]

    def pieces(c):
        tiles = feat // 128
        ends = [-(-tiles * (i + 1) // PIECES[c]) for i in range(PIECES[c])]
        starts = [0] + ends[:-1]
        return [pl.ds(128 * i, 128 * (j - i)) for i, j in zip(starts, ends)]

    def r3(c, p):
        f = pieces(c)[p]
        received(b_moves[c, p])

        def add(i, carry):
            side = x_back[c, 0, i, :, f].astype(F32) + x_back[c, 1, i, :, f].astype(F32)
            y_out[c, 1 - lo, i, :, f] = side.astype(BF16)
            same = x_buf[c, hi, core, lo, i, :, f]
            if c not in DIRECT:
                same = (same.astype(F32) + x_back[c, 2, i, :, f].astype(F32)).astype(BF16)
            y_out[c, lo, i, :, f] = same
            return carry

        lax.fori_loop(0, N_Y, add, 0)
        yb_moves[c, p] = [
            remote(y_out.at[c, :, (y + s) % N_Y, :, f], y_back.at[c, :, y, :, f], along_y(s))
            for s in (2, 1, 3)
        ]
        own_back[c, p] = [local(y_out.at[c, :, y, :, f], y_back.at[c, :, y, :, f])]
        if c in DIRECT:
            n = DIRECT.index(c)
            src = x_buf.at[c, 1 - hi, core, lo]
            yb_moves[c, p] += [
                remote(src.at[(y + s) % N_Y, :, f], far_back.at[n, y, :, f], along_y(s)) for s in (2, 1, 3)
            ]
            own_back[c, p].append(local(src.at[y, :, f], far_back.at[n, y, :, f]))

    def r4(c, p):
        f = pieces(c)[p]
        for copy in own_back[c, p]:
            copy.wait()
        received(yb_moves[c, p])
        rows = y_back[c, :, :, :, f]
        rows = rows.reshape(N_Y * N_LO * ROWS, rows.shape[-1])
        dims = (((0,), (0,)), ((), ()))
        total = lax.dot_general(mix_hi[c], rows, dims, preferred_element_type=F32)
        total = total + lax.dot_general(mix_lo[c], rows, dims, preferred_element_type=F32)
        total = total.reshape(2, n_tok, rows.shape[-1])
        for j, d in enumerate(CHUNKS[c]):
            behind = d + (1 if d > 0 else -1)
            part = total[j]
            if d and behind in MERGE:
                if p == 0:
                    received(m_moves[behind])
                part = part + merged[MERGE.index(behind), :, f].astype(F32)
            z_out[c, j, :, f] = part.astype(BF16)
            src = z_out.at[c, j, :, f]
            if d in MERGE:
                step = 1 if d > 0 else -1
                m_moves.setdefault(d, []).append(
                    remote(src, merged.at[MERGE.index(d), :, f], along_z(step))
                )
            elif d:
                zb_moves[c, j, p] = remote(src, z_back.at[c, j, :, f], along_z(d))
            else:
                own_z.append(local(src, z_back.at[c, j, :, f]))
        if c in DIRECT:
            n = DIRECT.index(c)
            at = pl.ds(pl.multiple_of(lo * n_rows, n_rows), n_rows)
            rows = far_back[n, :, :, f]
            rows = rows.reshape(n_rows, rows.shape[-1])
            total = lax.dot_general(mix_hi[c, at, :], rows, dims, preferred_element_type=F32)
            total = total + lax.dot_general(mix_lo[c, at, :], rows, dims, preferred_element_type=F32)
            far_out[n, :, :, f] = total.astype(BF16).reshape(2, n_tok, rows.shape[-1])
            for j, d in enumerate(CHUNKS[c]):
                src, dst = far_out.at[n, j, :, f], far_in.at[n, j, :, f]
                if d:
                    far_moves.append(remote(src, dst, along_z(d)))
                else:
                    far_own.append(local(src, dst))

    def fin():
        received(far_moves)
        for copy in far_own:
            copy.wait()

        def add(i, carry):
            at = pl.ds(pl.multiple_of(i * 16, 16), 16)
            total = jnp.zeros((16, feat), F32)
            for n in range(len(DIRECT)):
                for j in range(2):
                    total = total + far_in[n, j, at, :].astype(F32)
            swap_out[at, :] = total.astype(BF16)
            return carry

        lax.fori_loop(0, n_tok // 16, add, 0)
        swap_moves.append(remote(swap_out, swap_in, along_x(2)))

    own_z, own_back, m_moves, far_moves, far_own, swap_moves = [], {}, {}, [], [], []

    def own():
        for load in own_loads:
            load.wait()

    def load_weights():
        for load in weight_loads:
            load.wait()
        f = planned_of(expert)

        def pick_rows(i, carry):
            at = pl.ds(pl.multiple_of(i * 128, 128), 128)
            for w in (wg, wu):
                w[2, at, :] = (w[0, at, :].astype(F32) * (1.0 - f) + w[1, at, :].astype(F32) * f).astype(BF16)
            return carry

        lax.fori_loop(0, wg.shape[1] // 128, pick_rows, 0)

        def pick_down(i, carry):
            at = pl.ds(pl.multiple_of(i * 16, 16), 16)
            wd[2, at, :] = (wd[0, at, :].astype(F32) * (1.0 - f) + wd[1, at, :].astype(F32) * f).astype(BF16)
            return carry

        lax.fori_loop(0, hidden // 16, pick_down, 0)

    swap()
    z_near(0)
    z_near(-1)
    z_near(1)
    d1(0)
    z_far(0)
    d2(0)
    d1p(0)
    z_near(2)
    z_near(-2)
    d1(1)
    z_far(1)
    z_far(-1)
    d1f(0)
    load_weights()
    own()
    z_near(-3)
    z_near(3)
    d4(0)
    d1(2)
    d2(1)
    d1p(1)
    d3(0)
    d2(2)
    d1p(2)
    z_far(2)
    z_far(-2)
    d5(0)
    z_near(4)
    d1(3)
    r1(0)
    z_far(-3)
    z_far(3)
    d1f(2)
    d4(2)
    d1f(1)
    d4(1)
    d3(2)
    d2(3)
    z_far(4)
    d1f(3)
    d1p(3)
    r3(0, 0)
    d5(2)
    r1(2)
    r3(0, 1)
    d4(3)
    d3(3)
    d5(3)
    r4(0, 0)
    r3(2, 0)
    d3(1)
    r1(3)
    r4(0, 1)
    r3(2, 1)
    r4(2, 0)
    d5(1)
    r1(1)
    r3(3, 0)
    r4(2, 1)
    r3(3, 1)
    r4(3, 0)
    r4(3, 1)
    fin()
    r3(1, 0)
    r3(1, 1)
    r4(1, 0)
    r3(1, 2)
    r4(1, 1)
    r4(1, 2)
    for copy in own_z:
        copy.wait()
    received(zb_moves.values())
    received(swap_moves)

    def finish(i, carry):
        at = pl.ds(pl.multiple_of(i * 16, 16), 16)
        total = swap_in[at, :].astype(F32) if DIRECT else jnp.zeros((16, feat), F32)
        for c in range(n_chunk):
            for j in range(2):
                if CHUNKS[c][j] not in MERGE:
                    total = total + z_back[c, j, at, :].astype(F32)
        out_ref[at, :] = total.astype(out_ref.dtype)
        return carry

    lax.fori_loop(0, n_tok // 16, finish, 0)
    sent(list(started))


N_REMOTE = 23 + 4 * (9 + 2 + 4 + 1)
N_LOCAL = 4 + 4 * 3
for _c, _pair in enumerate(CHUNKS):
    _far = 1 + (_c in DIRECT)
    _away = sum(_d != 0 for _d in _pair)
    N_REMOTE += PIECES[_c] * (2 + (_c not in DIRECT) + _far * (3 + _away))
    N_LOCAL += PIECES[_c] * _far * (1 + (0 in _pair))


def per_device(tokens, expert_ids, gate_weights, replica_plan, w_gate, w_up, w_down):
    owners = lax.axis_size("expert")
    n_z = owners // (N_LO * N_Y)
    tok, feat = tokens.shape
    width = w_gate.shape[1]
    hidden = w_gate.shape[2]
    n_chunk = len(CHUNKS)
    vmem = pl.BlockSpec(memory_space=pltpu.VMEM)
    hbm = pl.BlockSpec(memory_space=pl.ANY)
    block = (N_Y, ROWS, feat)
    slot_rows = N_Y * N_LO * ROWS
    return pl.pallas_call(
        functools.partial(kernel, n_z),
        out_shape=jax.ShapeDtypeStruct((tok, feat), BF16),
        in_specs=[vmem, vmem, vmem, pl.BlockSpec(memory_space=pltpu.SMEM), hbm, hbm, hbm],
        out_specs=vmem,
        scratch_shapes=[
            pltpu.VMEM((3, width, hidden), BF16),
            pltpu.VMEM((3, width, hidden), BF16),
            pltpu.VMEM((3, hidden, width), BF16),
            pltpu.VMEM((n_chunk, N_HI, 2, tok, feat), BF16),
            pltpu.VMEM((n_chunk, 2, 16, tok), F32),
            pltpu.VMEM((16, tok), F32),
            pltpu.VMEM((n_chunk, slot_rows, 2 * tok), BF16),
            pltpu.VMEM((n_chunk, slot_rows, 2 * tok), BF16),
            pltpu.VMEM((n_chunk, slot_rows, 2 * tok), BF16),
            pltpu.VMEM((n_chunk, N_LO) + block, BF16),
            pltpu.VMEM((n_chunk,) + block, BF16),
            pltpu.VMEM((n_chunk,) + block, BF16),
            pltpu.VMEM((n_chunk, N_HI, N_CORE, N_LO) + block, BF16),
            pltpu.VMEM((n_chunk, N_HI, N_LO) + block, BF16),
            pltpu.VMEM((n_chunk, 3) + block, BF16),
            pltpu.VMEM((n_chunk, N_LO) + block, BF16),
            pltpu.VMEM((n_chunk, N_LO) + block, BF16),
            pltpu.VMEM((n_chunk, 2, tok, feat), BF16),
            pltpu.VMEM((n_chunk, 2, tok, feat), BF16),
            pltpu.VMEM((max(len(DIRECT), 1),) + block, BF16),
            pltpu.VMEM((max(len(DIRECT), 1), 2, tok, feat), BF16),
            pltpu.VMEM((max(len(DIRECT), 1), 2, tok, feat), BF16),
            pltpu.VMEM((max(len(MERGE), 1), tok, feat), BF16),
            pltpu.VMEM((tok, feat), BF16),
            pltpu.VMEM((tok, feat), BF16),
            pltpu.SemaphoreType.DMA((N_REMOTE,)),
            pltpu.SemaphoreType.DMA((N_REMOTE,)),
            pltpu.SemaphoreType.DMA((N_LOCAL,)),
        ],
        compiler_params=pltpu.CompilerParams(
            collective_id=0, has_side_effects=True, vmem_limit_bytes=67043328
        ),
    )(tokens, expert_ids.T, gate_weights.T, replica_plan, w_gate, w_up, w_down)


def solution(mesh):
    in_specs = (
        P("expert", "dp"),
        P("expert", None),
        P("expert", None),
        P(),
        P("expert", None, "dp"),
        P("expert", None, "dp"),
        P("expert", "dp", None),
    )
    return jax.shard_map(
        per_device, mesh=mesh, in_specs=in_specs, out_specs=P("expert", "dp"), check_vma=False
    )
```

```python
import functools

import jax
import jax.numpy as jnp
from jax import lax
from jax.experimental import pallas as pl
from jax.experimental.pallas import tpu as pltpu
from jax.sharding import PartitionSpec as P

CAP = 8
N_LO, N_Y, N_HI, N_CORE = 2, 4, 2, 2
N_X = N_LO * N_HI
GROUPS = 3
ROWS = GROUPS * 2 * CAP
CHUNKS = ((1, -1), (2, -2), (3, -3), (0, 4))
PIECES = (2, 3, 2, 2)
DIRECT = (0, 3, )
MERGE = (3, -3, 4, )
BF16, F32 = jnp.bfloat16, jnp.float32


def kernel(
    n_z, tok_ref, ids_ref, gate_ref, plan_ref, wg_hbm, wu_hbm, wd_hbm, out_ref,
    wg, wu, wd, toks, metas, meta_own, picks, mix_hi, mix_lo, g_buf, g_far, y_in, x_buf, core_in,
    x_back, y_out, y_back, z_out, z_back, far_back, far_out, far_in, merged, swap_out, swap_in,
    send_sem, recv_sem, local_sem,
):
    expert = lax.axis_index("expert")
    dp = lax.axis_index("dp")
    z, lo, y = expert // (N_LO * N_Y), (expert // N_Y) % N_LO, expert % N_Y
    hi, core = dp // N_CORE, dp % N_CORE
    x = hi * N_LO + lo
    n_tok = tok_ref.shape[0]
    feat = tok_ref.shape[1]
    hidden = wg.shape[2]
    n_chunk = len(CHUNKS)

    def device(z_, x_, y_, core_):
        return ((z_ * N_LO + x_ % N_LO) * N_Y + y_, (x_ // N_LO) * N_CORE + core_)

    def along_z(step):
        return device((z + step + n_z) % n_z, x, y, core)

    def along_y(step):
        return device(z, x, (y + step) % N_Y, core)

    def along_x(step):
        return device(z, (x + step) % N_X, y, core)

    right, left = (x + 1) % N_X, (x + N_X - 1) % N_X
    across = (x + 2) % N_X
    partner = device(z, x, y, 1 - core)

    started = []
    count = [0]
    local_count = [0]

    def remote(src, dst, target):
        i = count[0]
        count[0] += 1
        copy = pltpu.make_async_remote_copy(
            src_ref=src, dst_ref=dst, send_sem=send_sem.at[i], recv_sem=recv_sem.at[i],
            device_id=target, device_id_type=pl.DeviceIdType.MESH,
        )
        copy.start()
        started.append(copy)
        return copy

    def local(src, dst):
        i = local_count[0]
        local_count[0] += 1
        copy = pltpu.make_async_copy(src, dst, local_sem.at[i])
        copy.start()
        return copy

    def received(copies):
        for c in copies:
            c.wait_recv()

    def sent(copies):
        for c in copies:
            c.wait_send()
            started[:] = [other for other in started if other is not c]

    weight_loads = [
        local(wg_hbm, wg.at[pl.ds(0, 2)]),
        local(wu_hbm, wu.at[pl.ds(0, 2)]),
        local(wd_hbm, wd.at[pl.ds(0, 2)]),
    ]
    where = {d: (c, j) for c, pair in enumerate(CHUNKS) for j, d in enumerate(pair)}

    def tok_at(d, h):
        c, j = where[d]
        return toks.at[c, h, j]

    own_loads = [local(tok_ref, tok_at(0, hi))]
    meta_own[pl.ds(0, 8), :] = ids_ref[...].astype(F32)
    meta_own[pl.ds(8, 8), :] = gate_ref[...]
    metas[where[0]] = meta_own[...]

    barrier = pltpu.get_barrier_semaphore()
    peers = [along_z(s) for s in range(1, n_z)] + [along_y(s) for s in range(1, N_Y)]
    peers += [along_x(1), along_x(2), along_x(3), partner]
    for peer in peers:
        pl.semaphore_signal(barrier, inc=1, device_id=peer, device_id_type=pl.DeviceIdType.MESH)
    pl.semaphore_wait(barrier, len(peers))

    z_in, z_meta = {}, {}

    def z_near(d):
        for s in ((1, -1) if d == 0 else (1,) if d > 0 else (-1,)):
            if d:
                received([z_in[d, 0], z_meta[d]])
            nxt = d + s
            if nxt in where:
                src = tok_at(d, hi) if d else tok_ref
                src_m = metas.at[where[d]] if d else meta_own
                z_in[nxt, 0] = remote(src, tok_at(nxt, hi), along_z(-s))
                z_meta[nxt] = remote(src_m, metas.at[where[nxt]], along_z(-s))

    def z_far(d):
        received([z_in[d, 1]])
        for s in ((1, -1) if d == 0 else (1,) if d > 0 else (-1,)):
            nxt = d + s
            if nxt in where:
                z_in[nxt, 1] = remote(tok_at(d, 1 - hi), tok_at(nxt, 1 - hi), along_z(-s))

    def swap():
        z_in[0, 1] = remote(tok_ref, tok_at(0, hi), along_x(2))

    before = (
        lax.broadcasted_iota(jnp.int32, (n_tok, n_tok), 0)
        < lax.broadcasted_iota(jnp.int32, (n_tok, n_tok), 1)
    ).astype(F32).astype(BF16)
    plane = N_LO * N_Y
    place = lax.broadcasted_iota(jnp.int32, (CAP, n_tok), 0).astype(F32)
    blank = jnp.zeros((CAP, n_tok), F32)

    def planned_of(owner):
        owners = n_z * plane
        return (plan_ref[(owner + owners // 2) % owners] - 2 * owner).astype(F32)

    def slots(c):
        keys, gates = [], []
        ids = lax.broadcasted_iota(jnp.int32, (2 * plane, n_tok), 0) + z * (2 * plane)
        ids = ids.astype(F32)
        for j in range(2):
            meta = metas[c, j]
            member = jnp.zeros((2 * plane, n_tok), F32)
            gate = jnp.zeros((2 * plane, n_tok), F32)
            for k in range(8):
                hit = meta[k : k + 1, :] == ids
                member = jnp.where(hit, 1.0, member)
                gate = jnp.where(hit, meta[8 + k : 9 + k, :], gate)
            rank = jnp.dot(member.astype(BF16), before, preferred_element_type=F32)
            keys.append(jnp.where(member > 0.5, rank, -1.0))
            gates.append(gate)
        for yy in range(N_Y):
            for ll in range(N_LO):
                r = ll * (2 * N_Y) + yy * 2
                f = planned_of(z * plane + ll * N_Y + yy)
                base = (ll * N_Y + yy) * ROWS
                for g in range(GROUPS):
                    ones, weights = [], []
                    for j in range(2):
                        k0, k1 = keys[j][r : r + 1, :], keys[j][r + 1 : r + 2, :]
                        w0, w1 = gates[j][r : r + 1, :], gates[j][r + 1 : r + 2, :]
                        if g == 0:
                            k, w = k0, w0
                        elif g == 1:
                            k, w = k1, w1
                        else:
                            k = k0 * (1.0 - f) + k1 * f - float(CAP)
                            w = w0 * (1.0 - f) + w1 * f
                        hit = jnp.broadcast_to(k, (CAP, n_tok)) == place
                        one = jnp.where(hit, 1.0, 0.0)
                        weight = jnp.where(hit, jnp.broadcast_to(w, (CAP, n_tok)), 0.0)
                        row1 = [blank, blank]
                        row2 = [blank, blank]
                        row1[j], row2[j] = one, weight
                        ones.append(jnp.concatenate(row1, axis=1))
                        weights.append(jnp.concatenate(row2, axis=1))
                    at = pl.ds(base + g * 2 * CAP, 2 * CAP)
                    picks[c, at, :] = jnp.concatenate(ones, axis=0).astype(BF16)
                    w = jnp.concatenate(weights, axis=0)
                    high = w.astype(BF16)
                    mix_hi[c, at, :] = high
                    mix_lo[c, at, :] = (w - high.astype(F32)).astype(BF16)

    q_moves, p_moves, f_moves, x_moves, core_moves, own_moves = {}, {}, {}, {}, {}, {}
    reduce_moves, b_moves, yb_moves, zb_moves = {}, {}, {}, {}
    n_rows = N_Y * ROWS

    def to_planes(key, src, dst):
        moves = [remote(src((y + s) % N_Y), dst, along_y(s)) for s in (2, 1, 3)]
        own_moves[key] = local(src(y), dst)
        return moves

    def d1(c):
        slots(c)
        both = toks[c, hi].reshape(2 * n_tok, feat)
        rows = jnp.dot(picks[c], both, preferred_element_type=F32).astype(BF16)
        g_buf[c] = rows.reshape(N_LO, N_Y, ROWS, feat)
        q_moves[c] = to_planes((c, "q"), lambda t: g_buf.at[c, 1 - lo, t], y_in.at[c, y])

    def d1p(c):
        p_moves[c] = to_planes((c, "p"), lambda t: g_buf.at[c, lo, t], x_buf.at[c, hi, core, lo, y])

    def d1f(c):
        both = toks[c, 1 - hi].reshape(2 * n_tok, feat)
        at = pl.ds(pl.multiple_of(lo * n_rows, n_rows), n_rows)
        rows = jnp.dot(picks[c, at, :], both, preferred_element_type=F32).astype(BF16)
        g_far[c] = rows.reshape(N_Y, ROWS, feat)
        f_moves[c] = to_planes((c, "f"), lambda t: g_far.at[c, t], x_buf.at[c, 1 - hi, core, lo, y])

    def d2(c):
        own_moves[c, "q"].wait()
        received(q_moves[c])
        dst = x_buf.at[c, hi, core, lo]
        x_moves[c] = [remote(y_in.at[c], dst, along_x(1)), remote(y_in.at[c], dst, along_x(3))]

    def d3(c):
        own_moves[c, "p"].wait()
        received(p_moves[c])
        near = x_buf.at[c, hi, core, lo]
        core_moves.setdefault(c, []).append(remote(near, near, partner))
        own_moves[c, "f"].wait()
        received(f_moves[c])
        far = x_buf.at[c, 1 - hi, core, lo]
        core_moves[c].append(remote(far, far, partner))

    def d4(c):
        received(x_moves[c])
        for other in (left, right):
            block = x_buf.at[c, other // N_LO, core, 1 - lo]
            core_moves.setdefault(c, []).append(remote(block, block, partner))

    def d5(c):
        received(core_moves[c])
        sent(core_moves[c])

        def group(g, carry):
            at = pl.ds(pl.multiple_of(g * 2 * CAP, 2 * CAP), 2 * CAP)
            m = N_LO * N_Y * 2 * CAP
            gate = jnp.zeros((m, hidden), F32)
            up = jnp.zeros((m, hidden), F32)
            for q in range(4):
                rows = x_buf[c, q // 2, q % 2, :, :, at, :].reshape(m, feat)
                ks = pl.ds(q * feat, feat)
                gate += jnp.dot(rows, wg[g, ks, :], preferred_element_type=F32)
                up += jnp.dot(rows, wu[g, ks, :], preferred_element_type=F32)
            h = (gate / (1.0 + jnp.exp(-gate)) * up).astype(BF16)
            for q in range(4):
                o = jnp.dot(h, wd[g, :, pl.ds(q * feat, feat)], preferred_element_type=F32)
                x_buf[c, q // 2, q % 2, :, :, at, :] = o.astype(BF16).reshape(
                    N_LO, N_Y, 2 * CAP, feat
                )
            return carry

        lax.fori_loop(0, GROUPS, group, 0)
        reduce_moves[c] = remote(x_buf.at[c, :, 1 - core], core_in.at[c], partner)

    def r1(c):
        received([reduce_moves[c]])

        def add(i, carry):
            h_, s_, y_ = i // (N_LO * N_Y), (i // N_Y) % N_LO, i % N_Y
            total = x_buf[c, h_, core, s_, y_].astype(F32) + core_in[c, h_, s_, y_].astype(F32)
            x_buf[c, h_, core, s_, y_] = total.astype(BF16)
            return carry

        lax.fori_loop(0, N_HI * N_LO * N_Y, add, 0)
        for p, f in enumerate(pieces(c)):
            b_moves[c, p] = [
                remote(
                    x_buf.at[c, other // N_LO, core, par, :, :, f], x_back.at[c, i, :, :, f], along_x(step)
                )
                for i, (other, par, step) in enumerate(
                    ((right, 1 - lo, 1), (left, 1 - lo, 3), (across, lo, 2))[: 2 if c in DIRECT else 3]
                )
            ]

    def pieces(c):
        tiles = feat // 128
        ends = [-(-tiles * (i + 1) // PIECES[c]) for i in range(PIECES[c])]
        starts = [0] + ends[:-1]
        return [pl.ds(128 * i, 128 * (j - i)) for i, j in zip(starts, ends)]

    def r3(c, p):
        f = pieces(c)[p]
        received(b_moves[c, p])

        def add(i, carry):
            side = x_back[c, 0, i, :, f].astype(F32) + x_back[c, 1, i, :, f].astype(F32)
            y_out[c, 1 - lo, i, :, f] = side.astype(BF16)
            same = x_buf[c, hi, core, lo, i, :, f]
            if c not in DIRECT:
                same = (same.astype(F32) + x_back[c, 2, i, :, f].astype(F32)).astype(BF16)
            y_out[c, lo, i, :, f] = same
            return carry

        lax.fori_loop(0, N_Y, add, 0)
        yb_moves[c, p] = [
            remote(y_out.at[c, :, (y + s) % N_Y, :, f], y_back.at[c, :, y, :, f], along_y(s))
            for s in (2, 1, 3)
        ]
        own_back[c, p] = [local(y_out.at[c, :, y, :, f], y_back.at[c, :, y, :, f])]
        if c in DIRECT:
            n = DIRECT.index(c)
            src = x_buf.at[c, 1 - hi, core, lo]
            yb_moves[c, p] += [
                remote(src.at[(y + s) % N_Y, :, f], far_back.at[n, y, :, f], along_y(s)) for s in (2, 1, 3)
            ]
            own_back[c, p].append(local(src.at[y, :, f], far_back.at[n, y, :, f]))

    def r4(c, p):
        f = pieces(c)[p]
        for copy in own_back[c, p]:
            copy.wait()
        received(yb_moves[c, p])
        rows = y_back[c, :, :, :, f]
        rows = rows.reshape(N_Y * N_LO * ROWS, rows.shape[-1])
        dims = (((0,), (0,)), ((), ()))
        total = lax.dot_general(mix_hi[c], rows, dims, preferred_element_type=F32)
        total = total + lax.dot_general(mix_lo[c], rows, dims, preferred_element_type=F32)
        total = total.reshape(2, n_tok, rows.shape[-1])
        for j, d in enumerate(CHUNKS[c]):
            behind = d + (1 if d > 0 else -1)
            part = total[j]
            if d and behind in MERGE:
                if p == 0:
                    received(m_moves[behind])
                part = part + merged[MERGE.index(behind), :, f].astype(F32)
            z_out[c, j, :, f] = part.astype(BF16)
            src = z_out.at[c, j, :, f]
            if d in MERGE:
                step = 1 if d > 0 else -1
                m_moves.setdefault(d, []).append(
                    remote(src, merged.at[MERGE.index(d), :, f], along_z(step))
                )
            elif d:
                zb_moves[c, j, p] = remote(src, z_back.at[c, j, :, f], along_z(d))
            else:
                own_z.append(local(src, z_back.at[c, j, :, f]))
        if c in DIRECT:
            n = DIRECT.index(c)
            at = pl.ds(pl.multiple_of(lo * n_rows, n_rows), n_rows)
            rows = far_back[n, :, :, f]
            rows = rows.reshape(n_rows, rows.shape[-1])
            total = lax.dot_general(mix_hi[c, at, :], rows, dims, preferred_element_type=F32)
            total = total + lax.dot_general(mix_lo[c, at, :], rows, dims, preferred_element_type=F32)
            far_out[n, :, :, f] = total.astype(BF16).reshape(2, n_tok, rows.shape[-1])
            for j, d in enumerate(CHUNKS[c]):
                src, dst = far_out.at[n, j, :, f], far_in.at[n, j, :, f]
                if d:
                    far_moves.append(remote(src, dst, along_z(d)))
                else:
                    far_own.append(local(src, dst))

    def fin():
        received(far_moves)
        for copy in far_own:
            copy.wait()

        def add(i, carry):
            at = pl.ds(pl.multiple_of(i * 16, 16), 16)
            total = jnp.zeros((16, feat), F32)
            for n in range(len(DIRECT)):
                for j in range(2):
                    total = total + far_in[n, j, at, :].astype(F32)
            swap_out[at, :] = total.astype(BF16)
            return carry

        lax.fori_loop(0, n_tok // 16, add, 0)
        swap_moves.append(remote(swap_out, swap_in, along_x(2)))

    own_z, own_back, m_moves, far_moves, far_own, swap_moves = [], {}, {}, [], [], []

    def own():
        for load in own_loads:
            load.wait()

    def load_weights():
        for load in weight_loads:
            load.wait()
        f = planned_of(expert)

        def pick_rows(i, carry):
            at = pl.ds(pl.multiple_of(i * 128, 128), 128)
            for w in (wg, wu):
                w[2, at, :] = (w[0, at, :].astype(F32) * (1.0 - f) + w[1, at, :].astype(F32) * f).astype(BF16)
            return carry

        lax.fori_loop(0, wg.shape[1] // 128, pick_rows, 0)

        def pick_down(i, carry):
            at = pl.ds(pl.multiple_of(i * 16, 16), 16)
            wd[2, at, :] = (wd[0, at, :].astype(F32) * (1.0 - f) + wd[1, at, :].astype(F32) * f).astype(BF16)
            return carry

        lax.fori_loop(0, hidden // 16, pick_down, 0)

    swap()
    z_near(0)
    z_near(1)
    z_near(-1)
    d1(0)
    z_far(0)
    d2(0)
    z_near(2)
    d1p(0)
    load_weights()
    z_near(-2)
    d1(1)
    z_far(-1)
    z_far(1)
    d1f(0)
    own()
    z_near(-3)
    z_near(3)
    d2(1)
    d1(2)
    z_far(2)
    d1p(1)
    d2(2)
    z_near(4)
    d1(3)
    d3(0)
    d4(0)
    d4(1)
    d1p(2)
    z_far(3)
    z_far(-2)
    d2(3)
    d1p(3)
    d5(0)
    z_far(4)
    d4(2)
    d1f(3)
    z_far(-3)
    r1(0)
    d1f(2)
    d4(3)
    d3(3)
    d1f(1)
    d5(3)
    r3(0, 0)
    d3(2)
    r3(0, 1)
    d3(1)
    r1(3)
    d5(2)
    r4(0, 0)
    r3(3, 0)
    r1(2)
    r4(0, 1)
    d5(1)
    r3(3, 1)
    r4(3, 0)
    r3(2, 0)
    r1(1)
    r4(3, 1)
    r3(2, 1)
    r4(2, 0)
    r4(2, 1)
    r3(1, 0)
    r3(1, 1)
    r4(1, 0)
    r3(1, 2)
    r4(1, 1)
    fin()
    r4(1, 2)
    for copy in own_z:
        copy.wait()
    received(zb_moves.values())
    received(swap_moves)

    def finish(i, carry):
        at = pl.ds(pl.multiple_of(i * 16, 16), 16)
        total = swap_in[at, :].astype(F32) if DIRECT else jnp.zeros((16, feat), F32)
        for c in range(n_chunk):
            for j in range(2):
                if CHUNKS[c][j] not in MERGE:
                    total = total + z_back[c, j, at, :].astype(F32)
        out_ref[at, :] = total.astype(out_ref.dtype)
        return carry

    lax.fori_loop(0, n_tok // 16, finish, 0)
    sent(list(started))


N_REMOTE = 23 + 4 * (9 + 2 + 4 + 1)
N_LOCAL = 4 + 4 * 3
for _c, _pair in enumerate(CHUNKS):
    _far = 1 + (_c in DIRECT)
    _away = sum(_d != 0 for _d in _pair)
    N_REMOTE += PIECES[_c] * (2 + (_c not in DIRECT) + _far * (3 + _away))
    N_LOCAL += PIECES[_c] * _far * (1 + (0 in _pair))


def per_device(tokens, expert_ids, gate_weights, replica_plan, w_gate, w_up, w_down):
    owners = lax.axis_size("expert")
    n_z = owners // (N_LO * N_Y)
    tok, feat = tokens.shape
    width = w_gate.shape[1]
    hidden = w_gate.shape[2]
    n_chunk = len(CHUNKS)
    vmem = pl.BlockSpec(memory_space=pltpu.VMEM)
    hbm = pl.BlockSpec(memory_space=pl.ANY)
    block = (N_Y, ROWS, feat)
    slot_rows = N_Y * N_LO * ROWS
    return pl.pallas_call(
        functools.partial(kernel, n_z),
        out_shape=jax.ShapeDtypeStruct((tok, feat), BF16),
        in_specs=[vmem, vmem, vmem, pl.BlockSpec(memory_space=pltpu.SMEM), hbm, hbm, hbm],
        out_specs=vmem,
        scratch_shapes=[
            pltpu.VMEM((3, width, hidden), BF16),
            pltpu.VMEM((3, width, hidden), BF16),
            pltpu.VMEM((3, hidden, width), BF16),
            pltpu.VMEM((n_chunk, N_HI, 2, tok, feat), BF16),
            pltpu.VMEM((n_chunk, 2, 16, tok), F32),
            pltpu.VMEM((16, tok), F32),
            pltpu.VMEM((n_chunk, slot_rows, 2 * tok), BF16),
            pltpu.VMEM((n_chunk, slot_rows, 2 * tok), BF16),
            pltpu.VMEM((n_chunk, slot_rows, 2 * tok), BF16),
            pltpu.VMEM((n_chunk, N_LO) + block, BF16),
            pltpu.VMEM((n_chunk,) + block, BF16),
            pltpu.VMEM((n_chunk,) + block, BF16),
            pltpu.VMEM((n_chunk, N_HI, N_CORE, N_LO) + block, BF16),
            pltpu.VMEM((n_chunk, N_HI, N_LO) + block, BF16),
            pltpu.VMEM((n_chunk, 3) + block, BF16),
            pltpu.VMEM((n_chunk, N_LO) + block, BF16),
            pltpu.VMEM((n_chunk, N_LO) + block, BF16),
            pltpu.VMEM((n_chunk, 2, tok, feat), BF16),
            pltpu.VMEM((n_chunk, 2, tok, feat), BF16),
            pltpu.VMEM((max(len(DIRECT), 1),) + block, BF16),
            pltpu.VMEM((max(len(DIRECT), 1), 2, tok, feat), BF16),
            pltpu.VMEM((max(len(DIRECT), 1), 2, tok, feat), BF16),
            pltpu.VMEM((max(len(MERGE), 1), tok, feat), BF16),
            pltpu.VMEM((tok, feat), BF16),
            pltpu.VMEM((tok, feat), BF16),
            pltpu.SemaphoreType.DMA((N_REMOTE,)),
            pltpu.SemaphoreType.DMA((N_REMOTE,)),
            pltpu.SemaphoreType.DMA((N_LOCAL,)),
        ],
        compiler_params=pltpu.CompilerParams(
            collective_id=0, has_side_effects=True, vmem_limit_bytes=67043328
        ),
    )(tokens, expert_ids.T, gate_weights.T, replica_plan, w_gate, w_up, w_down)


def solution(mesh):
    in_specs = (
        P("expert", "dp"),
        P("expert", None),
        P("expert", None),
        P(),
        P("expert", None, "dp"),
        P("expert", None, "dp"),
        P("expert", "dp", None),
    )
    return jax.shard_map(
        per_device, mesh=mesh, in_specs=in_specs, out_specs=P("expert", "dp"), check_vma=False
    )
```
